256 devices in a mesh: group: 4 (over y_lo, core), inner: 64 (over x, z, y_hi).
Axes of the slice: x: 4, y: 4 (y_hi: 2, y_lo: 2; y = y_hi * 2 + y_lo), z: 8, core: 2. Of those that a mesh axis runs over, the one named last changes fastest.
Arguments:
- tokens: bfloat16 [256, 196, 1024], P('inner'), may hold values from -128 to 128
- output_grad: bfloat16 [256, 196, 1024], P('inner'), may hold values from -6 to 6
- router: bfloat16 [1024, 128], replicated, may hold values from -0.1890625 to 0.1890625
- weight_in: bfloat16 [128, 1024, 4096], P('inner', None, 'group'), may hold values from -0.1875 to 0.1875
- weight_out: bfloat16 [128, 4096, 1024], P('inner', 'group'), may hold values from -0.09375 to 0.09375
Outputs:
- token_grad: bfloat16 [256, 196, 1024], P('inner', None, 'group')
- router_grad: float32 [1024, 128], P('inner')
The draws below stay inside these ranges and needn't reach their ends.
All inputs are finite; a program needn't handle non-finite values.
Results may differ from the reference program's by a relative error of at most 0.015.
Values may be sent and summed in bfloat16 or wider, within the bound.
A program may use at most 64 MiB of HBM per device.

```python
import math
import jax
import jax.numpy as jnp
from jax import lax

D = 1024
FF = 4096
PATCHES = 196
IMAGES = 256
EXPERTS = 128


def router_values(key):
    drawn = jax.random.normal(jax.random.fold_in(key, 7), (D, EXPERTS), jnp.float32)
    return jnp.clip(drawn, -6.0, 6.0) / math.sqrt(D)


def draw_router(key, part):
    return router_values(key).astype(jnp.bfloat16)


def draw_tokens(key, part):
    base = jnp.clip(jax.random.normal(jax.random.fold_in(key, 11), (IMAGES, PATCHES, D), jnp.float32), -6.0, 6.0)
    return base.astype(jnp.bfloat16)


def block_levels(own_key, extent, cuts, low, top_value):
    loudness = 1.0
    for position, parts in cuts:
        draws = jax.random.uniform(jax.random.fold_in(jax.random.fold_in(own_key, 6), position), (parts,), jnp.float32, low / len(cuts), top_value / len(cuts))
        loudness = loudness * jnp.repeat(jnp.exp(draws), extent[position] // parts).reshape((-1,) + (1,) * (len(extent) - 1 - position))
    return loudness


def bell_draw(rng, shape, width, bound, pieces=(), held_as=jnp.bfloat16):
    entries = jax.random.normal(rng, shape, jnp.float32) * width
    if len(pieces) > 0:
        entries = block_levels(rng, shape, pieces, -0.22, 0.18) * entries
    return jnp.clip(entries, min=-bound, max=bound).astype(held_as)


def setup_inputs(seed: int = 0) -> dict:
    key_list = jax.random.split(jax.random.key(seed), 6)
    tokens = draw_tokens(jax.random.fold_in(key_list[5], 71), 0)
    output_grad = bell_draw(key_list[1], (IMAGES, PATCHES, D), 1.0, 6.0, ((0, 64),))
    router = draw_router(jax.random.fold_in(key_list[5], 71), 0)
    weight_in = bell_draw(key_list[3], (EXPERTS, D, FF), D ** -0.5, 0.1875, ((0, 64), (2, 4)))
    weight_out = bell_draw(key_list[4], (EXPERTS, FF, D), FF ** -0.5, 0.09375, ((0, 64), (1, 4)))
    return {"tokens": tokens, "output_grad": output_grad, "router": router, "weight_in": weight_in, "weight_out": weight_out}


def expert_backward(inputs):
    slot_x, slot_g, first, second = inputs
    pre_act = jnp.dot(slot_x, first, preferred_element_type=jnp.float32)
    activated, gelu_back = jax.vjp(jax.nn.gelu, pre_act)
    produced = jnp.dot(activated.astype(jnp.bfloat16), second, preferred_element_type=jnp.float32)
    act_grad = jnp.dot(slot_g, second.T, preferred_element_type=jnp.float32)
    pre_grad = gelu_back(act_grad)[0].astype(jnp.bfloat16)
    returned = jnp.dot(pre_grad, first.T, preferred_element_type=jnp.float32)
    return (produced.astype(jnp.bfloat16), returned.astype(jnp.bfloat16))

def reference(tokens, output_grad, router, weight_in, weight_out):
    token_wide = tokens.astype(jnp.float32)
    cot_wide = output_grad.astype(jnp.float32)
    router_wide = router.astype(jnp.float32)
    logits = jnp.einsum('bmd,ds->bms', token_wide, router_wide)
    dispatch = jax.nn.softmax(logits, axis=1)
    combine = jax.nn.softmax(logits, axis=2)
    dispatch_b = dispatch.astype(jnp.bfloat16)
    combine_b = combine.astype(jnp.bfloat16)
    slot_in = jnp.einsum('bms,bmd->bsd', dispatch_b.astype(jnp.float32), token_wide).astype(jnp.bfloat16)
    slot_grad = jnp.einsum('bms,bmd->bsd', combine_b.astype(jnp.float32), cot_wide).astype(jnp.bfloat16)
    produced, returned = lax.map(expert_backward, (jnp.transpose(slot_in, (1, 0, 2)), jnp.transpose(slot_grad, (1, 0, 2)), weight_in, weight_out))
    slot_out = jnp.transpose(produced, (1, 0, 2)).astype(jnp.float32)
    slot_back = jnp.transpose(returned, (1, 0, 2)).astype(jnp.float32)
    combine_grad = jnp.einsum('bmd,bsd->bms', cot_wide, slot_out)
    dispatch_grad = jnp.einsum('bmd,bsd->bms', token_wide, slot_back)
    logit_grad = combine * (combine_grad - lax.optimization_barrier(jnp.sum(combine * combine_grad, axis=2, keepdims=True)))
    logit_grad = logit_grad + dispatch * (dispatch_grad - lax.optimization_barrier(jnp.sum(dispatch * dispatch_grad, axis=1, keepdims=True)))
    logit_b = logit_grad.astype(jnp.bfloat16).astype(jnp.float32)
    token_grad = jnp.einsum('bms,bsd->bmd', dispatch_b.astype(jnp.float32), slot_back) + jnp.einsum('bms,ds->bmd', logit_b, router_wide)
    router_grad = jnp.einsum('bmd,bms->ds', token_wide, logit_b)
    return (token_grad.astype(jnp.bfloat16), router_grad)
```

```python
import functools
import math

import jax
import jax.numpy as jnp
from jax import lax
from jax.experimental import pallas as pl
from jax.experimental.pallas import tpu as pltpu
from jax.sharding import PartitionSpec as P

BF = jnp.bfloat16
F32 = jnp.float32
NX, NZ, NY = 4, 8, 2
NI = NX * NZ * NY
TOK = 196
PAD = 208
D = 1024
S = 128
NT = 512
CH = (3, 0, 2, 1)


def dz_of(k, p):
    if k == 0:
        return 4 * p
    return k if p == 0 else NZ - k


def dot(a, b, ca, cb):
    return lax.dot_general(a, b, (((ca,), (cb,)), ((), ())), preferred_element_type=F32)


def kernel(
    tok, og, router, w_in, w_out,
    tg_out, rg_out,
    win, wout, disp, comb, sbuf, x, fs, lhs, dg, act, pg, s0, s1,
    cbuf, pbuf, ybuf, rbuf, abuf, so, so_m, rgb, rr, tgb, qs,
    wsem, send1, recv1, ysend, yrecv, csend, crecv,
    psend, precv, bsend, brecv, asend, arecv,
    rsend, rrecv, qsend, qrecv, tsend, trecv,
):
    inner = lax.axis_index("inner")
    group = lax.axis_index("group")
    yh = lax.rem(inner, NY)
    zc = lax.rem(lax.div(inner, NY), NZ)
    xc = lax.div(inner, NY * NZ)
    yl = lax.div(group, 2)
    core = lax.rem(group, 2)

    def away(dx, dz, dy):
        x2, z2 = lax.rem(xc + dx, NX), lax.rem(zc + dz, NZ)
        y2, l2 = lax.rem(yh + dy, 2), lax.rem(yl + dy, 2)
        return (x2 * NZ + z2) * NY + y2, l2 * 2 + core

    def target(k, p, t, back):
        dx, dy, dz = lax.rem(t, NX), lax.div(t, NX), dz_of(k, p)
        if back:
            return away(NX - dx, NZ - dz, dy)
        return away(dx, dz, dy)

    def each_peer(fn, chunks=CH):
        for k in chunks:
            if k == 0:
                fn(0, 1, jnp.int32(0))
                lo = 1
            else:
                lo = 0

            @pl.loop(lo, 8)
            def _(t):
                fn(k, 0, t)
                fn(k, 1, t)

    def quad(j):
        return lax.rem(yl + j // 2, 2) * 2 + lax.rem(core + j % 2, 2)

    def dev(g, i):
        return {"group": g, "inner": i}

    barrier = pltpu.get_barrier_semaphore()

    def greet(k, p, t):
        i2, g2 = target(k, p, t, False)
        pl.semaphore_signal(barrier, inc=1, device_id=dev(g2, i2))

    each_peer(greet)
    for j in range(1, 4):
        pl.semaphore_signal(barrier, inc=1, device_id=dev(quad(j), inner))

    wcopy_in = pltpu.make_async_copy(w_in, win, wsem.at[0])
    wcopy_out = pltpu.make_async_copy(w_out, wout, wsem.at[1])
    wcopy_in.start()
    wcopy_out.start()

    logits = dot(tok[...], router[...], 1, 0)
    keep = lax.broadcasted_iota(jnp.int32, (PAD, S), 0) < TOK
    top = jnp.max(jnp.where(keep, logits, -jnp.inf), axis=0, keepdims=True)
    e = jnp.where(keep, jnp.exp(jnp.where(keep, logits - top, 0.0)), 0.0)
    disp[...] = e / jnp.sum(e, axis=0, keepdims=True)
    e = jnp.exp(logits - jnp.max(logits, axis=1, keepdims=True))
    comb[...] = e / jnp.sum(e, axis=1, keepdims=True)

    def to_tiles(kind, weights, values):
        flipped = weights.T.astype(BF)
        val = dot(flipped, values[...], 1, 0)
        for a in range(8):
            fs[pl.ds(a, S, stride=8), :] = val[:, a * 128 : (a + 1) * 128]
        sbuf[kind] = fs[...].reshape(S, 8, 128).astype(BF)

    def send_kind(kind):
        def send(k, p, t):
            i2, g2 = target(k, p, t, False)
            r = k * 16 + t * 2 + p
            pltpu.make_async_remote_copy(
                sbuf.at[kind, pl.ds(i2 * 2, 2)],
                x.at[kind, 0, r],
                send1.at[kind],
                recv1.at[kind, k],
                device_id=dev(g2, i2),
            ).start()

        pltpu.make_async_copy(
            sbuf.at[kind, pl.ds(inner * 2, 2)], x.at[kind, 0, 0], recv1.at[kind, 0]
        ).start()
        each_peer(send)

    to_tiles(0, disp[...], tok)
    pl.semaphore_wait(barrier, NI - 1 + 3)
    send_kind(0)
    to_tiles(1, comb[...], og)
    send_kind(1)

    def part(kind, q, k):
        return x.at[kind, q, pl.ds(k * 16, 16)]

    def ycopy(kind, k):
        return pltpu.make_async_remote_copy(
            part(kind, 0, k), part(kind, 1, k), ysend.at[kind, k], yrecv.at[kind, k],
            device_id=dev(quad(2), inner),
        )

    def ccopy(kind, q, k):
        return pltpu.make_async_remote_copy(
            part(kind, q, k), part(kind, q + 2, k), csend.at[kind, q, k], crecv.at[kind, q, k],
            device_id=dev(quad(1), inner),
        )

    def forward(kind):
        for k in CH:
            pltpu.make_async_copy(part(kind, 0, k), part(kind, 0, k), recv1.at[kind, k]).wait()
            ycopy(kind, k).start()
            ccopy(kind, 0, k).start()
        for k in CH:
            ycopy(kind, k).wait_recv()
            ccopy(kind, 1, k).start()

    def settle(kind):
        for q in range(2):
            for k in CH:
                ccopy(kind, q, k).wait_recv()

    def to_rows(kind, q):
        fs[...] = x[kind, q].astype(F32).reshape(1024, 128)
        for ex in range(2):
            for a in range(8):
                lhs[kind, ex, q * 64 : (q + 1) * 64, a * 128 : (a + 1) * 128] = fs[
                    pl.ds(ex * 8 + a, 64, stride=16), :
                ].astype(BF)

    def scatter_rows(dst, ex, n, val):
        for q in range(4):
            for a in range(NT // 128):
                dst[pl.ds(q * 1024 + ex * 8 + n * (NT // 128) + a, 64, stride=16), :] = val[
                    q * 64 : (q + 1) * 64, a * 128 : (a + 1) * 128
                ]

    c0 = math.sqrt(2.0 / math.pi)

    forward(0)
    to_rows(0, 0)
    to_rows(0, 1)
    settle(0)
    to_rows(0, 2)
    to_rows(0, 3)
    wcopy_in.wait()
    wcopy_out.wait()
    for ex in range(2):
        for n in range(D // NT):
            cols = slice(n * NT, (n + 1) * NT)
            h = dot(lhs[0, ex], win[ex, :, cols], 1, 0)
            h2 = h * h
            th = jnp.tanh(c0 * (h + 0.044715 * h2 * h))
            half = 0.5 * (1.0 + th)
            act[:, cols] = (h * half).astype(BF)
            dg[ex, :, cols] = half + 0.5 * h * (1.0 - th * th) * (
                c0 * (1.0 + (3.0 * 0.044715) * h2)
            )
        for n in range(D // NT):
            scatter_rows(s0, ex, n, dot(act[...], wout[ex, :, n * NT : (n + 1) * NT], 1, 0))

    def pcopy(kind, q):
        return pltpu.make_async_remote_copy(
            cbuf.at[kind, q], pbuf.at[kind, q], psend.at[kind, q], precv.at[kind, q],
            device_id=dev(quad(1), inner),
        )

    def bcopy(kind):
        return pltpu.make_async_remote_copy(
            ybuf.at[kind], rbuf.at[kind], bsend.at[kind], brecv.at[kind],
            device_id=dev(quad(2), inner),
        )

    def quarter(src, q):
        return src[q * 1024 : (q + 1) * 1024, :].reshape(64, 2, 8, 128)

    def reduce_1(kind, src):
        for q in (1, 0):
            cbuf[kind, q] = quarter(src, q + 2).astype(BF)
            pcopy(kind, q).start()

    def reduce_2(kind, src):
        pcopy(kind, 1).wait_recv()
        ybuf[kind] = (quarter(src, 1) + pbuf[kind, 1].astype(F32)).astype(BF)
        bcopy(kind).start()

    def reduce_3(kind, src):
        pcopy(kind, 0).wait_recv()
        bcopy(kind).wait_recv()
        abuf[kind] = (
            quarter(src, 0) + pbuf[kind, 0].astype(F32) + rbuf[kind].astype(F32)
        ).astype(BF)

        def send(k, p, t):
            i2, g2 = target(k, p, t, True)
            r = k * 16 + t * 2 + p
            pltpu.make_async_remote_copy(
                abuf.at[kind, r], so.at[kind, inner], asend.at[kind], arecv.at[kind],
                device_id=dev(g2, i2),
            ).start()

        pltpu.make_async_copy(abuf.at[kind, 0], so.at[kind, inner], arecv.at[kind]).start()
        each_peer(send)

    reduce_1(0, s0)
    forward(1)
    to_rows(1, 0)
    to_rows(1, 1)
    settle(1)
    to_rows(1, 2)
    to_rows(1, 3)
    reduce_2(0, s0)
    for ex in range(2):
        for n in range(D // NT):
            cols = slice(n * NT, (n + 1) * NT)
            ag = dot(lhs[1, ex], wout[ex, cols, :], 1, 1)
            pg[:, cols] = (dg[ex, :, cols] * ag).astype(BF)
        for n in range(D // NT):
            scatter_rows(s1, ex, n, dot(pg[...], win[ex, n * NT : (n + 1) * NT, :], 1, 1))
        if ex == 0:
            reduce_3(0, s0)
    reduce_1(1, s1)
    reduce_2(1, s1)
    reduce_3(1, s1)

    def gather_rows(kind):
        pltpu.make_async_copy(so.at[kind], so.at[kind], arecv.at[kind]).wait()
        fs[...] = so[kind].astype(F32).reshape(1024, 128)
        for a in range(8):
            so_m[kind, :, a * 128 : (a + 1) * 128] = fs[pl.ds(a, S, stride=8), :].astype(BF)

    gather_rows(0)
    cg = dot(og[...], so_m[0], 1, 1)
    cw = comb[...]
    lg = cw * (cg - jnp.sum(cw * cg, axis=1, keepdims=True))
    gather_rows(1)
    dgr = dot(tok[...], so_m[1], 1, 1)
    dw = disp[...]
    lg = lg + dw * (dgr - jnp.sum(dw * dgr, axis=0, keepdims=True))
    lb = lg.astype(BF)
    rgb[...] = dot(tok[...], lb, 0, 0).astype(BF).reshape(NI, 16, 128)

    def send_router(k, p, t):
        i2, g2 = target(k, p, t, False)
        r = k * 16 + t * 2 + p
        pltpu.make_async_remote_copy(
            rgb.at[i2], rr.at[r], rsend, rrecv, device_id=dev(g2, i2)
        ).start()

    pltpu.make_async_copy(rgb.at[inner], rr.at[0], rrecv).start()
    each_peer(send_router)

    tg = dot(dw.astype(BF), so_m[1], 1, 0) + dot(lb, router[...], 1, 1)
    for g in range(4):
        tgb[g] = tg[:, g * 256 : (g + 1) * 256].astype(BF)

    def tcopy(j):
        g2 = quad(j)
        return pltpu.make_async_remote_copy(
            tgb.at[g2], tg_out.at[group], tsend.at[j], trecv.at[j], device_id=dev(g2, inner)
        )

    for j in (2, 3, 1):
        tcopy(j).start()
    mine = pltpu.make_async_copy(tgb.at[group], tg_out.at[group], tsend.at[0])
    mine.start()

    pltpu.make_async_copy(rr, rr, rrecv).wait()
    qs[0] = jnp.sum(rr[...].astype(F32), axis=0)

    def qcopy(j):
        return pltpu.make_async_remote_copy(
            qs.at[0], qs.at[j], qsend.at[j], qrecv.at[j], device_id=dev(quad(j), inner)
        )

    for j in (2, 3, 1):
        qcopy(j).start()
    for j in range(1, 4):
        tcopy(j).wait()
    mine.wait()
    for j in range(1, 4):
        qcopy(j).wait()
    rg_out[...] = (qs[0] + qs[1]) + (qs[2] + qs[3])

    for kind in range(2):
        pltpu.make_async_copy(
            x.at[kind, 0, pl.ds(1, NI - 1)], x.at[kind, 0, pl.ds(1, NI - 1)], send1.at[kind]
        ).wait()
        pltpu.make_async_copy(
            so.at[kind, pl.ds(1, NI - 1)], so.at[kind, pl.ds(1, NI - 1)], asend.at[kind]
        ).wait()
        for k in CH:
            ycopy(kind, k).wait_send()
            for q in range(2):
                ccopy(kind, q, k).wait_send()
        for q in range(2):
            pcopy(kind, q).wait_send()
        bcopy(kind).wait_send()
    pltpu.make_async_copy(rr.at[pl.ds(1, NI - 1)], rr.at[pl.ds(1, NI - 1)], rsend).wait()


def local(tokens, output_grad, router, weight_in, weight_out):
    g = lax.axis_index("group")

    def mine(a):
        one = lax.dynamic_index_in_dim(a, g, 0, keepdims=False)
        return jnp.pad(one, ((0, PAD - TOK), (0, 0)))

    dma = pltpu.SemaphoreType.DMA
    vm = pl.BlockSpec(memory_space=pltpu.VMEM)
    hbm = pl.BlockSpec(memory_space=pl.ANY)
    tg, rg = pl.pallas_call(
        kernel,
        name="moe_backward",
        out_shape=(
            jax.ShapeDtypeStruct((4, PAD, 256), BF),
            jax.ShapeDtypeStruct((16, S), F32),
        ),
        in_specs=[vm, vm, vm, hbm, hbm],
        out_specs=(vm, vm),
        scratch_shapes=[
            pltpu.VMEM((2, D, D), BF),
            pltpu.VMEM((2, D, D), BF),
            pltpu.VMEM((PAD, S), F32),
            pltpu.VMEM((PAD, S), F32),
            pltpu.VMEM((2, S, 8, 128), BF),
            pltpu.VMEM((2, 4, NI, 2, 8, 128), BF),
            pltpu.VMEM((1024, 128), F32),
            pltpu.VMEM((2, 2, 256, D), BF),
            pltpu.VMEM((2, 256, D), F32),
            pltpu.VMEM((256, D), BF),
            pltpu.VMEM((256, D), BF),
            pltpu.VMEM((4096, 128), F32),
            pltpu.VMEM((4096, 128), F32),
            pltpu.VMEM((2, 2, NI, 2, 8, 128), BF),
            pltpu.VMEM((2, 2, NI, 2, 8, 128), BF),
            pltpu.VMEM((2, NI, 2, 8, 128), BF),
            pltpu.VMEM((2, NI, 2, 8, 128), BF),
            pltpu.VMEM((2, NI, 2, 8, 128), BF),
            pltpu.VMEM((2, NI, 2, 8, 128), BF),
            pltpu.VMEM((2, S, D), BF),
            pltpu.VMEM((NI, 16, 128), BF),
            pltpu.VMEM((NI, 16, 128), BF),
            pltpu.VMEM((4, PAD, 256), BF),
            pltpu.VMEM((4, 16, 128), F32),
            dma((2,)),
            dma((2,)), dma((2, 4)),
            dma((2, 4)), dma((2, 4)),
            dma((2, 2, 4)), dma((2, 2, 4)),
            dma((2, 2)), dma((2, 2)),
            dma((2,)), dma((2,)),
            dma((2,)), dma((2,)),
            dma, dma,
            dma((4,)), dma((4,)),
            dma((4,)), dma((4,)),
        ],
        compiler_params=pltpu.CompilerParams(
            collective_id=0, has_side_effects=True, vmem_limit_bytes=58 * 1024 * 1024
        ),
    )(mine(tokens), mine(output_grad), router, weight_in, weight_out)
    return tg[:, :TOK], rg


def solution(mesh):
    return jax.shard_map(
        local,
        mesh=mesh,
        in_specs=(
            P("inner", None, None),
            P("inner", None, None),
            P(),
            P("inner", None, "group"),
            P("inner", "group", None),
        ),
        out_specs=(P("inner", None, "group"), P("inner", None)),
        check_vma=False,
    )
```

```python
import contextlib
import math

import jax
import jax.numpy as jnp
from jax import lax
from jax.experimental import pallas as pl
from jax.experimental.pallas import tpu as pltpu
from jax.sharding import PartitionSpec as P

BF = jnp.bfloat16
F32 = jnp.float32
NX, NZ, NY = 4, 8, 2
NI = NX * NZ * NY
TOK = 196
PAD = 208
D = 1024
S = 128
RAW = TOK * 32
NT = 512
CH = (3, 0, 2, 1)


def scope(name):
    return contextlib.nullcontext()


def dz_of(k, p):
    if k == 0:
        return 4 * p
    return k if p == 0 else NZ - k


def dot(a, b, ca, cb):
    return lax.dot_general(a, b, (((ca,), (cb,)), ((), ())), preferred_element_type=F32)


def kernel(
    tok_all, og_all, router, w_in, w_out,
    tg_out, rg_out,
    raw, wide, tok, og, land, win, wout, disp, comb, sbuf, x, fs, lhs, dg, act, pg, s0, s1,
    cbuf, pbuf, ybuf, rbuf, abuf, so, so_m, rgo, rgs, rgp, rgb, rr, tgb, qs,
    tsem, wsem, send1, recv1, ysend, yrecv, csend, crecv,
    psend, precv, bsend, brecv, asend, arecv,
    gsend, grecv, rsend, rrecv, qsend, qrecv, tsend, trecv,
):
    inner = lax.axis_index("inner")
    group = lax.axis_index("group")
    yh = lax.rem(inner, NY)
    zc = lax.rem(lax.div(inner, NY), NZ)
    xc = lax.div(inner, NY * NZ)
    yl = lax.div(group, 2)
    core = lax.rem(group, 2)

    def away(dx, dz, dy):
        x2, z2 = lax.rem(xc + dx, NX), lax.rem(zc + dz, NZ)
        y2, l2 = lax.rem(yh + dy, 2), lax.rem(yl + dy, 2)
        return (x2 * NZ + z2) * NY + y2, l2 * 2 + core

    def target(k, p, t, back):
        dx, dy, dz = lax.rem(t, NX), lax.div(t, NX), dz_of(k, p)
        if back:
            return away(NX - dx, NZ - dz, dy)
        return away(dx, dz, dy)

    def each_peer(fn, chunks=CH):
        for k in chunks:
            if k == 0:
                fn(0, 1, jnp.int32(0))
                lo = 1
            else:
                lo = 0

            @pl.loop(lo, 8)
            def _(t):
                fn(k, 0, t)
                fn(k, 1, t)

    def quad(j):
        return lax.rem(yl + j // 2, 2) * 2 + lax.rem(core + j % 2, 2)

    def dev(g, i):
        return {"group": g, "inner": i}

    barrier = pltpu.get_barrier_semaphore()

    def greet(k, p, t):
        i2, g2 = target(k, p, t, False)
        pl.semaphore_signal(barrier, inc=1, device_id=dev(g2, i2))

    each_peer(greet)
    for j in range(1, 4):
        pl.semaphore_signal(barrier, inc=1, device_id=dev(quad(j), inner))

    def fetch(kind, n):
        src = (tok_all, og_all)[kind]
        rows = pl.ds(n * (RAW // 4), RAW // 4)
        return pltpu.make_async_copy(src.at[rows], raw.at[kind, rows], tsem.at[kind, n])

    for kind in range(2):
        for n in range(4):
            fetch(kind, n).start()
    wcopy_in = pltpu.make_async_copy(w_in, win, wsem.at[0])
    wcopy_out = pltpu.make_async_copy(w_out, wout, wsem.at[1])
    wcopy_in.start()
    wcopy_out.start()

    wide[RAW:, :] = jnp.zeros((PAD * 32 - RAW, 128), F32)

    def extract(kind, dst):
        for n in range(4):
            fetch(kind, n).wait()
            rows = slice(n * (RAW // 4), (n + 1) * (RAW // 4))
            wide[rows, :] = raw[kind, rows, :].astype(F32)
        for a in range(8):
            dst[:, a * 128 : (a + 1) * 128] = wide[
                pl.ds(a * 4 + group, PAD, stride=32), :
            ].astype(BF)

    with scope("extract0"):
        extract(0, tok)
    logits = dot(tok[...], router[...], 1, 0)
    keep = lax.broadcasted_iota(jnp.int32, (PAD, S), 0) < TOK
    top = jnp.max(jnp.where(keep, logits, -jnp.inf), axis=0, keepdims=True)
    e = jnp.where(keep, jnp.exp(jnp.where(keep, logits - top, 0.0)), 0.0)
    disp[...] = e / jnp.sum(e, axis=0, keepdims=True)
    e = jnp.exp(logits - jnp.max(logits, axis=1, keepdims=True))
    comb[...] = e / jnp.sum(e, axis=1, keepdims=True)

    def to_tiles(kind, weights, values):
        flipped = weights.T.astype(BF)
        val = dot(flipped, values[...], 1, 0)
        for a in range(8):
            fs[pl.ds(a, S, stride=8), :] = val[:, a * 128 : (a + 1) * 128]
        sbuf[kind] = fs[...].reshape(S, 8, 128).astype(BF)

    def send_kind(kind):
        def send(k, p, t):
            i2, g2 = target(k, p, t, False)
            r = k * 16 + t * 2 + p
            pltpu.make_async_remote_copy(
                sbuf.at[kind, pl.ds(i2 * 2, 2)],
                x.at[kind, 0, r],
                send1.at[kind],
                recv1.at[kind, k],
                device_id=dev(g2, i2),
            ).start()

        pltpu.make_async_copy(
            sbuf.at[kind, pl.ds(inner * 2, 2)], x.at[kind, 0, 0], recv1.at[kind, 0]
        ).start()
        each_peer(send)

    with scope("tiles0"):
        to_tiles(0, disp[...], tok)
    with scope("barrier"):
        pl.semaphore_wait(barrier, NI - 1 + 3)
    with scope("send0"):
        send_kind(0)
    with scope("extract1"):
        extract(1, og)
    with scope("tiles1"):
        to_tiles(1, comb[...], og)
    with scope("send1"):
        send_kind(1)

    def part(kind, q, k):
        return x.at[kind, q, pl.ds(k * 16, 16)]

    def ycopy(kind, k):
        return pltpu.make_async_remote_copy(
            part(kind, 0, k), part(kind, 1, k), ysend.at[kind, k], yrecv.at[kind, k],
            device_id=dev(quad(2), inner),
        )

    def ccopy(kind, q, k):
        return pltpu.make_async_remote_copy(
            part(kind, q, k), part(kind, q + 2, k), csend.at[kind, q, k], crecv.at[kind, q, k],
            device_id=dev(quad(1), inner),
        )

    def forward_a(kind, k):
        pltpu.make_async_copy(part(kind, 0, k), part(kind, 0, k), recv1.at[kind, k]).wait()
        ycopy(kind, k).start()
        ccopy(kind, 0, k).start()

    def forward_b(kind, k):
        ycopy(kind, k).wait_recv()
        ccopy(kind, 1, k).start()

    def settle(kind):
        for q in range(2):
            for k in CH:
                ccopy(kind, q, k).wait_recv()

    def to_rows(kind, q):
        fs[...] = x[kind, q].astype(F32).reshape(1024, 128)
        for ex in range(2):
            for a in range(8):
                lhs[kind, ex, q * 64 : (q + 1) * 64, a * 128 : (a + 1) * 128] = fs[
                    pl.ds(ex * 8 + a, 64, stride=16), :
                ].astype(BF)

    def scatter_rows(dst, ex, n, val):
        for q in range(4):
            for a in range(NT // 128):
                dst[pl.ds(q * 1024 + ex * 8 + n * (NT // 128) + a, 64, stride=16), :] = val[
                    q * 64 : (q + 1) * 64, a * 128 : (a + 1) * 128
                ]

    c0 = math.sqrt(2.0 / math.pi)

    def pcopy(kind, q):
        return pltpu.make_async_remote_copy(
            cbuf.at[kind, q], pbuf.at[kind, q], psend.at[kind, q], precv.at[kind, q],
            device_id=dev(quad(1), inner),
        )

    def bcopy(kind, k):
        sel = pl.ds(k * 16, 16)
        return pltpu.make_async_remote_copy(
            ybuf.at[kind, sel], rbuf.at[kind, sel], bsend.at[kind, k], brecv.at[kind, k],
            device_id=dev(quad(2), inner),
        )

    def quarter(src, q):
        return src[q * 1024 : (q + 1) * 1024, :].reshape(64, 2, 8, 128)

    def reduce_1(kind, src):
        for q in (1, 0):
            cbuf[kind, q] = quarter(src, q + 2).astype(BF)
            pcopy(kind, q).start()

    def chunk(src, q, k):
        return src[q * 1024 + k * 256 : q * 1024 + (k + 1) * 256, :].reshape(16, 2, 8, 128)

    def reduce_2(kind, src):
        pcopy(kind, 1).wait_recv()
        for k in CH:
            sel = pl.ds(k * 16, 16)
            ybuf[kind, sel] = (chunk(src, 1, k) + pbuf[kind, 1, sel].astype(F32)).astype(BF)
            bcopy(kind, k).start()
        pcopy(kind, 0).wait_recv()
        src[0:1024, :] = src[0:1024, :] + pbuf[kind, 0].astype(F32).reshape(1024, 128)

    def reduce_3(kind, src, k):
        sel = pl.ds(k * 16, 16)
        bcopy(kind, k).wait_recv()
        abuf[kind, sel] = (chunk(src, 0, k) + rbuf[kind, sel].astype(F32)).astype(BF)
        if k == 0:
            pltpu.make_async_copy(abuf.at[kind, 0], so.at[kind, inner], arecv.at[kind]).start()

        def send(k, p, t):
            i2, g2 = target(k, p, t, True)
            pltpu.make_async_remote_copy(
                abuf.at[kind, k * 16 + t * 2 + p], so.at[kind, inner], asend.at[kind],
                arecv.at[kind], device_id=dev(g2, i2),
            ).start()

        each_peer(send, (k,))

    def pre(ex):
        for n in range(D // NT):
            cols = slice(n * NT, (n + 1) * NT)
            h = dot(lhs[0, ex], win[ex, :, cols], 1, 0)
            h2 = h * h
            th = jnp.tanh(c0 * (h + 0.044715 * h2 * h))
            half = 0.5 * (1.0 + th)
            act[:, cols] = (h * half).astype(BF)
            dg[ex, :, cols] = half + 0.5 * h * (1.0 - th * th) * (
                c0 * (1.0 + (3.0 * 0.044715) * h2)
            )

    def out(ex):
        for n in range(D // NT):
            scatter_rows(s0, ex, n, dot(act[...], wout[ex, :, n * NT : (n + 1) * NT], 1, 0))

    def act_grad(ex):
        for n in range(D // NT):
            cols = slice(n * NT, (n + 1) * NT)
            ag = dot(lhs[1, ex], wout[ex, cols, :], 1, 1)
            pg[:, cols] = (dg[ex, :, cols] * ag).astype(BF)

    def back(ex):
        for n in range(D // NT):
            scatter_rows(s1, ex, n, dot(pg[...], win[ex, n * NT : (n + 1) * NT, :], 1, 1))

    with scope("fwdA0"):
        for k in CH:
            forward_a(0, k)
    with scope("fwdA1_0"):
        forward_a(1, CH[0])
    with scope("fwdB0"):
        for k in CH:
            forward_b(0, k)
    with scope("rows0ab"):
        to_rows(0, 0)
        to_rows(0, 1)
    with scope("settle0"):
        settle(0)
    with scope("rows0cd"):
        to_rows(0, 2)
        to_rows(0, 3)
    with scope("fwdA1_1"):
        forward_a(1, CH[1])
    wcopy_in.wait()
    wcopy_out.wait()
    with scope("pre"):
        pre(0)
    with scope("fwdA1_2"):
        forward_a(1, CH[2])
    with scope("out"):
        out(0)
    with scope("fwdA1_3"):
        forward_a(1, CH[3])
    with scope("pre"):
        pre(1)
    with scope("fwdB1"):
        forward_b(1, CH[0])
    with scope("out"):
        out(1)
    with scope("reduce1_0"):
        reduce_1(0, s0)
    with scope("fwdB1"):
        for k in CH[1:]:
            forward_b(1, k)
    with scope("reduce2_0"):
        reduce_2(0, s0)
    with scope("rows1ab"):
        to_rows(1, 0)
        to_rows(1, 1)
    with scope("settle1"):
        settle(1)
    with scope("rows1cd"):
        to_rows(1, 2)
        to_rows(1, 3)
    for ex in range(2):
        with scope("actgrad"):
            act_grad(ex)
        with scope("back"):
            back(ex)
    with scope("reduce1_1"):
        reduce_1(1, s1)
    with scope("reduce3_0"):
        reduce_3(0, s0, CH[0])
    with scope("reduce2_1"):
        reduce_2(1, s1)
    for k in CH[1:]:
        with scope("reduce3_0"):
            reduce_3(0, s0, k)
    for k in CH:
        with scope("reduce3_1"):
            reduce_3(1, s1, k)

    def gather_rows(kind):
        pltpu.make_async_copy(so.at[kind], so.at[kind], arecv.at[kind]).wait()
        fs[...] = so[kind].astype(F32).reshape(1024, 128)
        for a in range(8):
            so_m[kind, :, a * 128 : (a + 1) * 128] = fs[pl.ds(a, S, stride=8), :].astype(BF)

    with scope("gather0"):
        gather_rows(0)
    cg = dot(og[...], so_m[0], 1, 1)
    cw = comb[...]
    lg = cw * (cg - jnp.sum(cw * cg, axis=1, keepdims=True))
    with scope("gather1"):
        gather_rows(1)
    dgr = dot(tok[...], so_m[1], 1, 1)
    dw = disp[...]
    lg = lg + dw * (dgr - jnp.sum(dw * dgr, axis=0, keepdims=True))
    lb = lg.astype(BF)
    rg = dot(tok[...], lb, 0, 0).reshape(NI, 2, 8, 128)
    rgo[...] = rg
    rgs[...] = rgo[:, pl.ds(1 - core, 1)].reshape(NI, 8, 128).astype(BF)

    gcopy = pltpu.make_async_remote_copy(
        rgs, rgp, gsend, grecv, device_id=dev(quad(1), inner)
    )
    gcopy.start()
    with scope("tg"):
        tg = dot(dw.astype(BF), so_m[1], 1, 0) + dot(lb, router[...], 1, 1)
        for g in range(4):
            tgb[g] = tg[:, g * 256 : (g + 1) * 256].astype(BF)

    def tcopy(j):
        g2 = quad(j)
        return pltpu.make_async_remote_copy(
            tgb.at[g2], land.at[group], tsend.at[j], trecv.at[j], device_id=dev(g2, inner)
        )

    gcopy.wait_recv()
    rgb[...] = (
        rgo[:, pl.ds(core, 1)].reshape(NI, 8, 128) + rgp[...].astype(F32)
    ).astype(BF)

    def send_router(k, p, t):
        i2, g2 = target(k, p, t, False)
        pltpu.make_async_remote_copy(
            rgb.at[i2], rr.at[k * 16 + t * 2 + p], rsend, rrecv, device_id=dev(g2, i2)
        ).start()

    with scope("send_router"):
        pltpu.make_async_copy(rgb.at[inner], rr.at[0], rrecv).start()
        each_peer(send_router)
    for j in (2, 3, 1):
        tcopy(j).start()
    mine = pltpu.make_async_copy(tgb.at[group], land.at[group], tsend.at[0])
    mine.start()

    with scope("wait_tg"):
        for j in range(1, 4):
            tcopy(j).wait()
        mine.wait()
    with scope("tg_out"):
        for g in range(4):
            for a in range(2):
                wide[pl.ds(a * 4 + g, PAD, stride=8), :] = land[
                    g, :, a * 128 : (a + 1) * 128
                ].astype(F32)
        tg_out[...] = wide[: TOK * 8, :].astype(BF)

    with scope("wait_router"):
        pltpu.make_async_copy(rr, rr, rrecv).wait()
    qs[0] = jnp.sum(rr[...].astype(F32), axis=0)

    def qcopy(j):
        return pltpu.make_async_remote_copy(
            qs.at[0], qs.at[j], qsend.at[j], qrecv.at[j], device_id=dev(quad(j), inner)
        )

    for j in (2, 3, 1):
        qcopy(j).start()
    with scope("wait_q"):
        for j in range(1, 4):
            qcopy(j).wait()
    rg_out[pl.ds(core * 8, 8), :] = qs[0] + qs[2]
    rg_out[pl.ds((1 - core) * 8, 8), :] = qs[1] + qs[3]

    for kind in range(2):
        pltpu.make_async_copy(
            x.at[kind, 0, pl.ds(1, NI - 1)], x.at[kind, 0, pl.ds(1, NI - 1)], send1.at[kind]
        ).wait()
        pltpu.make_async_copy(
            so.at[kind, pl.ds(1, NI - 1)], so.at[kind, pl.ds(1, NI - 1)], asend.at[kind]
        ).wait()
        for k in CH:
            ycopy(kind, k).wait_send()
            for q in range(2):
                ccopy(kind, q, k).wait_send()
        for q in range(2):
            pcopy(kind, q).wait_send()
        for k in CH:
            bcopy(kind, k).wait_send()
    gcopy.wait_send()
    pltpu.make_async_copy(rr.at[pl.ds(1, NI - 1)], rr.at[pl.ds(1, NI - 1)], rsend).wait()


def local(tokens, output_grad, router, weight_in, weight_out):
    def as_stored(a):
        a = a.transpose(1, 0, 2).reshape(TOK, 4, 8, 128).transpose(0, 2, 1, 3)
        return a.reshape(RAW, 128)

    dma = pltpu.SemaphoreType.DMA
    vm = pl.BlockSpec(memory_space=pltpu.VMEM)
    hbm = pl.BlockSpec(memory_space=pl.ANY)
    tg, rg = pl.pallas_call(
        kernel,
        name="moe_backward",
        out_shape=(
            jax.ShapeDtypeStruct((TOK * 8, 128), BF),
            jax.ShapeDtypeStruct((16, S), F32),
        ),
        in_specs=[hbm, hbm, vm, hbm, hbm],
        out_specs=(vm, vm),
        scratch_shapes=[
            pltpu.VMEM((2, RAW, 128), BF),
            pltpu.VMEM((PAD * 32, 128), F32),
            pltpu.VMEM((PAD, D), BF),
            pltpu.VMEM((PAD, D), BF),
            pltpu.VMEM((4, PAD, 256), BF),
            pltpu.VMEM((2, D, D), BF),
            pltpu.VMEM((2, D, D), BF),
            pltpu.VMEM((PAD, S), F32),
            pltpu.VMEM((PAD, S), F32),
            pltpu.VMEM((2, S, 8, 128), BF),
            pltpu.VMEM((2, 4, NI, 2, 8, 128), BF),
            pltpu.VMEM((1024, 128), F32),
            pltpu.VMEM((2, 2, 256, D), BF),
            pltpu.VMEM((2, 256, D), F32),
            pltpu.VMEM((256, D), BF),
            pltpu.VMEM((256, D), BF),
            pltpu.VMEM((4096, 128), F32),
            pltpu.VMEM((4096, 128), F32),
            pltpu.VMEM((2, 2, NI, 2, 8, 128), BF),
            pltpu.VMEM((2, 2, NI, 2, 8, 128), BF),
            pltpu.VMEM((2, NI, 2, 8, 128), BF),
            pltpu.VMEM((2, NI, 2, 8, 128), BF),
            pltpu.VMEM((2, NI, 2, 8, 128), BF),
            pltpu.VMEM((2, NI, 2, 8, 128), BF),
            pltpu.VMEM((2, S, D), BF),
            pltpu.VMEM((NI, 2, 8, 128), F32),
            pltpu.VMEM((NI, 8, 128), BF),
            pltpu.VMEM((NI, 8, 128), BF),
            pltpu.VMEM((NI, 8, 128), BF),
            pltpu.VMEM((NI, 8, 128), BF),
            pltpu.VMEM((4, PAD, 256), BF),
            pltpu.VMEM((4, 8, 128), F32),
            dma((2, 4)),
            dma((2,)),
            dma((2,)), dma((2, 4)),
            dma((2, 4)), dma((2, 4)),
            dma((2, 2, 4)), dma((2, 2, 4)),
            dma((2, 2)), dma((2, 2)),
            dma((2, 4)), dma((2, 4)),
            dma((2,)), dma((2,)),
            dma, dma,
            dma, dma,
            dma((4,)), dma((4,)),
            dma((4,)), dma((4,)),
        ],
        compiler_params=pltpu.CompilerParams(
            collective_id=0, has_side_effects=True, vmem_limit_bytes=58 * 1024 * 1024
        ),
    )(as_stored(tokens), as_stored(output_grad), router, weight_in, weight_out)
    tg = tg.reshape(TOK, 2, 4, 128).transpose(2, 0, 1, 3).reshape(4, TOK, 256)
    return tg, rg


def solution(mesh):
    return jax.shard_map(
        local,
        mesh=mesh,
        in_specs=(
            P("inner", None, None),
            P("inner", None, None),
            P(),
            P("inner", None, "group"),
            P("inner", "group", None),
        ),
        out_specs=(P("inner", None, "group"), P("inner", None)),
        check_vma=False,
    )
```

```python
import contextlib
import math

import jax
import jax.numpy as jnp
from jax import lax
from jax.experimental import pallas as pl
from jax.experimental.pallas import tpu as pltpu
from jax.sharding import PartitionSpec as P

BF = jnp.bfloat16
F32 = jnp.float32
NX, NZ, NY = 4, 8, 2
NI = NX * NZ * NY
TOK = 196
PAD = 208
D = 1024
S = 128
RAW = TOK * 32
NT = 512
CH = (3, 0, 2, 1)
HALVES = ((3, 0), (2, 1))
SELF = 16


def scope(name):
    return contextlib.nullcontext()


def slot_of(k, p, t):
    return CH.index(k) * 16 + t * 2 + p


def dz_of(k, p):
    if k == 0:
        return 4 * p
    return k if p == 0 else NZ - k


def dot(a, b, ca, cb):
    return lax.dot_general(a, b, (((ca,), (cb,)), ((), ())), preferred_element_type=F32)


def kernel(
    tok_all, og_all, router_all, w_in, w_out,
    land, rg,
    raw, wide, tok, og, router, win, wout, disp, comb, sbuf, x, fs, lhs, dg, act, pg, s0, s1, s2, s3,
    cbuf, pbuf, ybuf, rbuf, abuf, so, so_m, rgo, rgs, rgp, rgb, rr, tgb, qs,
    tsem, wsem, send1, recv1, ysend, yrecv, csend, crecv,
    psend, precv, bsend, brecv, asend, arecv,
    gsend, grecv, rsend, rrecv, qsend, qrecv, tsend, trecv,
):
    inner = lax.axis_index("inner")
    group = lax.axis_index("group")
    yh = lax.rem(inner, NY)
    zc = lax.rem(lax.div(inner, NY), NZ)
    xc = lax.div(inner, NY * NZ)
    yl = lax.div(group, 2)
    core = lax.rem(group, 2)

    def away(dx, dz, dy):
        x2, z2 = lax.rem(xc + dx, NX), lax.rem(zc + dz, NZ)
        y2, l2 = lax.rem(yh + dy, 2), lax.rem(yl + dy, 2)
        return (x2 * NZ + z2) * NY + y2, l2 * 2 + core

    def target(k, p, t, back):
        dx, dy, dz = lax.rem(t, NX), lax.div(t, NX), dz_of(k, p)
        if back:
            return away(NX - dx, NZ - dz, dy)
        return away(dx, dz, dy)

    def each_peer(fn, chunks=CH):
        for k in chunks:
            if k == 0:
                fn(0, 1, jnp.int32(0))
                lo = 1
            else:
                lo = 0

            @pl.loop(lo, 8)
            def _(t):
                fn(k, 0, t)
                fn(k, 1, t)

    def quad(j):
        return lax.rem(yl + j // 2, 2) * 2 + lax.rem(core + j % 2, 2)

    def dev(g, i):
        return {"group": g, "inner": i}

    def fetch(kind, n):
        src = (tok_all, og_all)[kind]
        rows = pl.ds(n * (RAW // 4), RAW // 4)
        return pltpu.make_async_copy(src.at[rows], raw.at[kind, rows], tsem.at[kind, n])

    router_copy = pltpu.make_async_copy(router_all, router, wsem.at[2])
    for n in range(4):
        fetch(0, n).start()
    router_copy.start()
    for n in range(4):
        fetch(1, n).start()
    barrier = pltpu.get_barrier_semaphore()

    def greet(k, p, t):
        i2, g2 = target(k, p, t, False)
        pl.semaphore_signal(barrier, inc=1, device_id=dev(g2, i2))

    each_peer(greet)
    for j in range(1, 4):
        pl.semaphore_signal(barrier, inc=1, device_id=dev(quad(j), inner))

    wcopy_in = pltpu.make_async_copy(w_in, win, wsem.at[0])
    wcopy_out = pltpu.make_async_copy(w_out, wout, wsem.at[1])
    wcopy_in.start()
    wcopy_out.start()

    wide[RAW:, :] = jnp.zeros((PAD * 32 - RAW, 128), F32)

    def extract(kind, dst):
        for n in range(4):
            fetch(kind, n).wait()
            rows = slice(n * (RAW // 4), (n + 1) * (RAW // 4))
            wide[rows, :] = raw[kind, rows, :].astype(F32)
        for a in range(8):
            dst[:, a * 128 : (a + 1) * 128] = wide[
                pl.ds(a * 4 + group, PAD, stride=32), :
            ].astype(BF)

    with scope("extract0"):
        extract(0, tok)
    router_copy.wait()
    logits = dot(tok[...], router[...], 1, 0)
    keep = lax.broadcasted_iota(jnp.int32, (PAD, S), 0) < TOK
    top = jnp.max(jnp.where(keep, logits, -jnp.inf), axis=0, keepdims=True)
    e = jnp.where(keep, jnp.exp(jnp.where(keep, logits - top, 0.0)), 0.0)
    disp[...] = e / jnp.sum(e, axis=0, keepdims=True)
    e = jnp.exp(logits - jnp.max(logits, axis=1, keepdims=True))
    comb[...] = e / jnp.sum(e, axis=1, keepdims=True)

    def to_tiles(kind, weights, values):
        flipped = weights.T.astype(BF)
        val = dot(flipped, values[...], 1, 0)
        for a in range(8):
            fs[pl.ds(a, S, stride=8), :] = val[:, a * 128 : (a + 1) * 128]
        sbuf[kind] = fs[...].reshape(S, 8, 128).astype(BF)

    def send_stage(st):
        kind, ex = st // 2, st % 2

        def send(k, p, t):
            i2, g2 = target(k, p, t, False)
            pltpu.make_async_remote_copy(
                sbuf.at[kind, i2 * 2 + ex],
                x.at[st, 0, slot_of(k, p, t)],
                send1.at[st],
                recv1.at[st, CH.index(k) // 2],
                device_id=dev(g2, i2),
            ).start()

        pltpu.make_async_copy(
            sbuf.at[kind, inner * 2 + ex], x.at[st, 0, SELF], recv1.at[st, 0]
        ).start()
        each_peer(send)

    with scope("tiles0"):
        to_tiles(0, disp[...], tok)
    with scope("barrier"):
        pl.semaphore_wait(barrier, NI - 1 + 3)
    with scope("send0"):
        send_stage(0)
        send_stage(1)
    with scope("extract1"):
        extract(1, og)
    with scope("tiles1"):
        to_tiles(1, comb[...], og)
    with scope("send1"):
        send_stage(2)
        send_stage(3)

    def part(st, q, h):
        return x.at[st, q, pl.ds(h * 32, 32)]

    def ycopy(st, h):
        return pltpu.make_async_remote_copy(
            part(st, 0, h), part(st, 1, h), ysend.at[st, h], yrecv.at[st, h],
            device_id=dev(quad(2), inner),
        )

    def ccopy(st, q, h):
        return pltpu.make_async_remote_copy(
            part(st, q, h), part(st, q + 2, h), csend.at[st, q, h], crecv.at[st, q, h],
            device_id=dev(quad(1), inner),
        )

    def forward_a(st, h):
        with scope(f"fwdA{st}{h}"):
            pltpu.make_async_copy(part(st, 0, h), part(st, 0, h), recv1.at[st, h]).wait()
        ycopy(st, h).start()
        ccopy(st, 0, h).start()

    def forward_b(st, h):
        with scope(f"fwdB{st}{h}"):
            ycopy(st, h).wait_recv()
        ccopy(st, 1, h).start()

    def to_rows(st, q):
        fs[0:512, :] = x[st, q].astype(F32).reshape(512, 128)
        for a in range(8):
            lhs[st, q * 64 : (q + 1) * 64, a * 128 : (a + 1) * 128] = fs[
                pl.ds(a, 64, stride=8), :
            ].astype(BF)

    def rows_ab(st):
        to_rows(st, 0)
        to_rows(st, 1)

    def rows_cd(st):
        for q in range(2):
            with scope(f"settle{st}{q}"):
                for h in range(2):
                    ccopy(st, q, h).wait_recv()
            to_rows(st, q + 2)

    def scatter_rows(dst, n, val):
        for q in range(4):
            for a in range(NT // 128):
                dst[pl.ds(q * 512 + n * (NT // 128) + a, 64, stride=8), :] = val[
                    q * 64 : (q + 1) * 64, a * 128 : (a + 1) * 128
                ]

    sums = (s0, s1, s2, s3)
    c0 = math.sqrt(2.0 / math.pi)

    def pre(ex):
        for n in range(D // NT):
            cols = slice(n * NT, (n + 1) * NT)
            h = dot(lhs[ex], win[ex, :, cols], 1, 0)
            h2 = h * h
            th = jnp.tanh(c0 * (h + 0.044715 * h2 * h))
            half = 0.5 * (1.0 + th)
            act[:, cols] = (h * half).astype(BF)
            dg[ex, :, cols] = half + 0.5 * h * (1.0 - th * th) * (
                c0 * (1.0 + (3.0 * 0.044715) * h2)
            )

    def out(ex):
        for n in range(D // NT):
            scatter_rows(sums[ex], n, dot(act[...], wout[ex, :, n * NT : (n + 1) * NT], 1, 0))

    def act_grad(ex):
        for n in range(D // NT):
            cols = slice(n * NT, (n + 1) * NT)
            ag = dot(lhs[2 + ex], wout[ex, cols, :], 1, 1)
            pg[:, cols] = (dg[ex, :, cols] * ag).astype(BF)

    def back(ex):
        for n in range(D // NT):
            scatter_rows(
                sums[2 + ex], n, dot(pg[...], win[ex, n * NT : (n + 1) * NT, :], 1, 1)
            )

    def pcopy(st, q):
        return pltpu.make_async_remote_copy(
            cbuf.at[st, q], pbuf.at[st, q], psend.at[st, q], precv.at[st, q],
            device_id=dev(quad(1), inner),
        )

    def bcopy(st, h):
        sel = pl.ds(h * 32, 32)
        return pltpu.make_async_remote_copy(
            ybuf.at[st, sel], rbuf.at[st, sel], bsend.at[st, h], brecv.at[st, h],
            device_id=dev(quad(2), inner),
        )

    def rows_of(st, q, h):
        lo = q * 512 + h * 256
        return sums[st][lo : lo + 256, :].reshape(32, 8, 128)

    def reduce_1(st):
        with scope(f"reduce1_{st}"):
            for q in (1, 0):
                cbuf[st, q] = (
                    sums[st][(q + 2) * 512 : (q + 3) * 512, :].reshape(64, 8, 128).astype(BF)
                )
                pcopy(st, q).start()

    def reduce_2(st):
        with scope(f"reduce2_{st}"):
            pcopy(st, 1).wait_recv()
            for h in range(2):
                sel = pl.ds(h * 32, 32)
                ybuf[st, sel] = (rows_of(st, 1, h) + pbuf[st, 1, sel].astype(F32)).astype(BF)
                bcopy(st, h).start()
            pcopy(st, 0).wait_recv()

    def reduce_3(st, h):
        kind, ex = st // 2, st % 2
        sel = pl.ds(h * 32, 32)
        with scope(f"reduce3_{st}{h}"):
            bcopy(st, h).wait_recv()
        abuf[st, sel] = (
            rows_of(st, 0, h) + pbuf[st, 0, sel].astype(F32) + rbuf[st, sel].astype(F32)
        ).astype(BF)
        if h == 0:
            pltpu.make_async_copy(
                abuf.at[st, SELF], so.at[kind, inner, ex], arecv.at[kind]
            ).start()

        def send(k, p, t):
            i2, g2 = target(k, p, t, True)
            pltpu.make_async_remote_copy(
                abuf.at[st, slot_of(k, p, t)], so.at[kind, inner, ex], asend.at[st],
                arecv.at[kind], device_id=dev(g2, i2),
            ).start()

        with scope("a2a"):
            each_peer(send, HALVES[h])

    forward_a(0, 0)
    forward_a(0, 1)
    forward_a(1, 0)
    forward_b(0, 0)
    forward_a(1, 1)
    forward_b(0, 1)
    with scope("rows"):
        rows_ab(0)
    forward_a(2, 0)
    with scope("rows"):
        rows_cd(0)
    wcopy_in.wait()
    wcopy_out.wait()
    with scope("pre"):
        pre(0)
    forward_b(1, 0)
    forward_a(2, 1)
    forward_b(1, 1)
    with scope("out"):
        out(0)
    reduce_1(0)
    forward_a(3, 0)
    with scope("rows"):
        rows_ab(1)
        rows_cd(1)
    reduce_2(0)
    with scope("pre"):
        pre(1)
    forward_b(2, 0)
    forward_a(3, 1)
    with scope("out"):
        out(1)
    reduce_1(1)
    forward_b(2, 1)
    with scope("rows"):
        rows_ab(2)
        rows_cd(2)
    reduce_2(1)
    with scope("actgrad"):
        act_grad(0)
    forward_b(3, 0)
    with scope("back"):
        back(0)
    reduce_1(2)
    forward_b(3, 1)
    with scope("rows"):
        rows_ab(3)
    reduce_3(0, 0)
    with scope("rows"):
        rows_cd(3)
    reduce_2(2)
    with scope("actgrad"):
        act_grad(1)
    reduce_3(0, 1)
    with scope("back"):
        back(1)
    reduce_1(3)
    reduce_3(1, 0)
    reduce_2(3)
    reduce_3(1, 1)
    for st in (2, 3):
        for h in range(2):
            reduce_3(st, h)

    def gather_rows(kind):
        pltpu.make_async_copy(so.at[kind], so.at[kind], arecv.at[kind]).wait()
        fs[...] = so[kind].astype(F32).reshape(1024, 128)
        for a in range(8):
            so_m[kind, :, a * 128 : (a + 1) * 128] = fs[pl.ds(a, S, stride=8), :].astype(BF)

    with scope("gather0"):
        gather_rows(0)
    cg = dot(og[...], so_m[0], 1, 1)
    cw = comb[...]
    lg = cw * (cg - jnp.sum(cw * cg, axis=1, keepdims=True))
    with scope("gather1"):
        gather_rows(1)
    dgr = dot(tok[...], so_m[1], 1, 1)
    dw = disp[...]
    lg = lg + dw * (dgr - jnp.sum(dw * dgr, axis=0, keepdims=True))
    lb = lg.astype(BF)
    rgo[...] = dot(tok[...], lb, 0, 0).reshape(NI, 2, 8, 128)
    rgs[...] = rgo[:, pl.ds(1 - core, 1)].reshape(NI, 8, 128).astype(BF)

    gcopy = pltpu.make_async_remote_copy(
        rgs, rgp, gsend, grecv, device_id=dev(quad(1), inner)
    )
    gcopy.start()
    with scope("tg"):
        tg = dot(dw.astype(BF), so_m[1], 1, 0) + dot(lb, router[...], 1, 1)
        for g in range(4):
            tgb[g] = tg[:, g * 256 : (g + 1) * 256].astype(BF)

    def tcopy(j):
        g2 = quad(j)
        return pltpu.make_async_remote_copy(
            tgb.at[g2], land.at[group], tsend.at[j], trecv.at[j], device_id=dev(g2, inner)
        )

    for j in (2, 3, 1):
        tcopy(j).start()
    mine = pltpu.make_async_copy(tgb.at[group], land.at[group], tsend.at[0])
    mine.start()

    with scope("wait_g"):
        gcopy.wait_recv()
    rgb[...] = (
        rgo[:, pl.ds(core, 1)].reshape(NI, 8, 128) + rgp[...].astype(F32)
    ).astype(BF)

    def send_router(k, p, t):
        i2, g2 = target(k, p, t, False)
        pltpu.make_async_remote_copy(
            rgb.at[i2], rr.at[slot_of(k, p, t)], rsend, rrecv, device_id=dev(g2, i2)
        ).start()

    with scope("send_router"):
        pltpu.make_async_copy(rgb.at[inner], rr.at[SELF], rrecv).start()
        each_peer(send_router)

    with scope("wait_router"):
        pltpu.make_async_copy(rr, rr, rrecv).wait()
    qs[0] = jnp.sum(rr[...].astype(F32), axis=0)

    def qcopy(j):
        return pltpu.make_async_remote_copy(
            qs.at[0], qs.at[j], qsend.at[j], qrecv.at[j], device_id=dev(quad(j), inner)
        )

    for j in (2, 3, 1):
        qcopy(j).start()
    with scope("wait_tg"):
        for j in range(1, 4):
            tcopy(j).wait()
        mine.wait()
    with scope("wait_q"):
        for j in range(1, 4):
            qcopy(j).wait()
    rg[pl.ds(core * 8, 8), :] = qs[0] + qs[2]
    rg[pl.ds((1 - core) * 8, 8), :] = qs[1] + qs[3]

    for st in range(4):
        pltpu.make_async_copy(
            x.at[st, 0, pl.ds(1, NI - 1)], x.at[st, 0, pl.ds(1, NI - 1)], send1.at[st]
        ).wait()
        pltpu.make_async_copy(
            abuf.at[st, pl.ds(1, NI - 1)], abuf.at[st, pl.ds(1, NI - 1)], asend.at[st]
        ).wait()
        for h in range(2):
            ycopy(st, h).wait_send()
            bcopy(st, h).wait_send()
            for q in range(2):
                ccopy(st, q, h).wait_send()
        for q in range(2):
            pcopy(st, q).wait_send()
    gcopy.wait_send()
    pltpu.make_async_copy(rr.at[pl.ds(1, NI - 1)], rr.at[pl.ds(1, NI - 1)], rsend).wait()


def finish(land, rg, tg_out, rg_out, wide):
    for g in range(4):
        for a in range(2):
            wide[pl.ds(a * 4 + g, PAD, stride=8), :] = land[
                g, :, a * 128 : (a + 1) * 128
            ].astype(F32)
    tg_out[...] = wide[: TOK * 8, :].astype(BF)
    rg_out[...] = rg[...]


def local(tokens, output_grad, router, weight_in, weight_out):
    def as_stored(a):
        a = a.transpose(1, 0, 2).reshape(TOK, 4, 8, 128).transpose(0, 2, 1, 3)
        return a.reshape(RAW, 128)

    dma = pltpu.SemaphoreType.DMA
    vm = pl.BlockSpec(memory_space=pltpu.VMEM)
    hbm = pl.BlockSpec(memory_space=pl.ANY)
    land, rg = pl.pallas_call(
        kernel,
        name="moe_backward",
        out_shape=(pltpu.VMEM((4, PAD, 256), BF), pltpu.VMEM((16, S), F32)),
        in_specs=[hbm, hbm, hbm, hbm, hbm],
        out_specs=(vm, vm),
        scratch_shapes=[
            pltpu.VMEM((2, RAW, 128), BF),
            pltpu.VMEM((PAD * 32, 128), F32),
            pltpu.VMEM((PAD, D), BF),
            pltpu.VMEM((PAD, D), BF),
            pltpu.VMEM((D, S), BF),
            pltpu.VMEM((2, D, D), BF),
            pltpu.VMEM((2, D, D), BF),
            pltpu.VMEM((PAD, S), F32),
            pltpu.VMEM((PAD, S), F32),
            pltpu.VMEM((2, S, 8, 128), BF),
            pltpu.VMEM((4, 4, NI, 8, 128), BF),
            pltpu.VMEM((1024, 128), F32),
            pltpu.VMEM((4, 256, D), BF),
            pltpu.VMEM((2, 256, D), F32),
            pltpu.VMEM((256, D), BF),
            pltpu.VMEM((256, D), BF),
            pltpu.VMEM((2048, 128), F32),
            pltpu.VMEM((2048, 128), F32),
            pltpu.VMEM((2048, 128), F32),
            pltpu.VMEM((2048, 128), F32),
            pltpu.VMEM((4, 2, NI, 8, 128), BF),
            pltpu.VMEM((4, 2, NI, 8, 128), BF),
            pltpu.VMEM((4, NI, 8, 128), BF),
            pltpu.VMEM((4, NI, 8, 128), BF),
            pltpu.VMEM((4, NI, 8, 128), BF),
            pltpu.VMEM((2, NI, 2, 8, 128), BF),
            pltpu.VMEM((2, S, D), BF),
            pltpu.VMEM((NI, 2, 8, 128), F32),
            pltpu.VMEM((NI, 8, 128), BF),
            pltpu.VMEM((NI, 8, 128), BF),
            pltpu.VMEM((NI, 8, 128), BF),
            pltpu.VMEM((NI, 8, 128), BF),
            pltpu.VMEM((4, PAD, 256), BF),
            pltpu.VMEM((4, 8, 128), F32),
            dma((2, 4)),
            dma((3,)),
            dma((4,)), dma((4, 2)),
            dma((4, 2)), dma((4, 2)),
            dma((4, 2, 2)), dma((4, 2, 2)),
            dma((4, 2)), dma((4, 2)),
            dma((4, 2)), dma((4, 2)),
            dma((4,)), dma((2,)),
            dma, dma,
            dma, dma,
            dma((4,)), dma((4,)),
            dma((4,)), dma((4,)),
        ],
        compiler_params=pltpu.CompilerParams(
            collective_id=0, has_side_effects=True, vmem_limit_bytes=58 * 1024 * 1024
        ),
    )(as_stored(tokens), as_stored(output_grad), router, weight_in, weight_out)
    tg, rg = pl.pallas_call(
        finish,
        name="moe_finish",
        out_shape=(
            jax.ShapeDtypeStruct((TOK * 8, 128), BF),
            jax.ShapeDtypeStruct((16, S), F32),
        ),
        in_specs=[vm, vm],
        out_specs=(vm, vm),
        scratch_shapes=[pltpu.VMEM((PAD * 8, 128), F32)],
        compiler_params=pltpu.CompilerParams(vmem_limit_bytes=16 * 1024 * 1024),
    )(land, rg)
    tg = tg.reshape(TOK, 2, 4, 128).transpose(2, 0, 1, 3).reshape(4, TOK, 256)
    return tg, rg


def solution(mesh):
    return jax.shard_map(
        local,
        mesh=mesh,
        in_specs=(
            P("inner", None, None),
            P("inner", None, None),
            P(),
            P("inner", None, "group"),
            P("inner", "group", None),
        ),
        out_specs=(P("inner", None, "group"), P("inner", None)),
        check_vma=False,
    )
```

```python
import contextlib
import math

import jax
import jax.numpy as jnp
from jax import lax
from jax.experimental import pallas as pl
from jax.experimental.pallas import tpu as pltpu
from jax.sharding import PartitionSpec as P

BF = jnp.bfloat16
F32 = jnp.float32
NX, NZ, NY = 4, 8, 2
NI = NX * NZ * NY
TOK = 196
PAD = 208
D = 1024
S = 128
RAW = TOK * 32
NT = 512
NEAR, FAR = 0, 1
DZ = ((0, 1, 7, 2), (4, 3, 5, 6))
SELF = 0


def scope(name):
    return contextlib.nullcontext()


def dot(a, b, ca, cb):
    return lax.dot_general(a, b, (((ca,), (cb,)), ((), ())), preferred_element_type=F32)


def kernel(
    tok_all, og_all, router_all, w_in, w_out,
    tg_out, rg,
    raw, wide, tok, og, router, land, win, wout, disp, comb, sbuf, x, fs, lhs, dg, act, pg, s0, s1, s2, s3,
    cbuf, pbuf, ybuf, rbuf, abuf, so, so_m, rgo, rgs, rgp, rgb, rr, tgb, qs,
    tsem, wsem, send1, recv1, ysend, yrecv, csend, crecv,
    psend, precv, bsend, brecv, asend, arecv,
    gsend, grecv, rsend, rrecv, qsend, qrecv, tsend, trecv,
):
    inner = lax.axis_index("inner")
    group = lax.axis_index("group")
    yh = lax.rem(inner, NY)
    zc = lax.rem(lax.div(inner, NY), NZ)
    xc = lax.div(inner, NY * NZ)
    yl = lax.div(group, 2)
    core = lax.rem(group, 2)

    ahead = [lax.rem(zc + dz, NZ) * NY for dz in range(NZ)]
    behind = [lax.rem(zc + NZ - dz, NZ) * NY for dz in range(NZ)]

    def each_peer(fn, half, back=False):
        def at(t, js):
            dx, dy = lax.rem(t, NX), lax.div(t, NX)
            x2 = lax.rem(xc + (NX - dx if back else dx), NX) * (NY * NZ)
            y2, l2 = lax.rem(yh + dy, 2), lax.rem(yl + dy, 2)
            base, g2 = x2 + y2, l2 * 2 + core
            for j in js:
                dz = DZ[half][j]
                fn(base + (behind if back else ahead)[dz], g2, half * 32 + j * 8 + t)

        lo = 0
        if half == NEAR:
            at(jnp.int32(0), (1, 2, 3))
            lo = 1

        @pl.loop(lo, 8)
        def _(t):
            at(t, (0, 1, 2, 3))

    def quad(j):
        return lax.rem(yl + j // 2, 2) * 2 + lax.rem(core + j % 2, 2)

    def dev(g, i):
        return {"group": g, "inner": i}

    def fetch(kind, n):
        src = (tok_all, og_all)[kind]
        rows = pl.ds(n * (RAW // 4), RAW // 4)
        return pltpu.make_async_copy(src.at[rows], raw.at[kind, rows], tsem.at[kind, n])

    router_copy = pltpu.make_async_copy(router_all, router, wsem.at[2])
    for n in range(4):
        fetch(0, n).start()
    router_copy.start()
    for n in range(4):
        fetch(1, n).start()
    barrier = pltpu.get_barrier_semaphore()

    def greet(i2, g2, r):
        pl.semaphore_signal(barrier, inc=1, device_id=dev(g2, i2))

    each_peer(greet, FAR)
    each_peer(greet, NEAR)
    for j in range(1, 4):
        pl.semaphore_signal(barrier, inc=1, device_id=dev(quad(j), inner))

    wcopy_in = pltpu.make_async_copy(w_in, win, wsem.at[0])
    wcopy_out = pltpu.make_async_copy(w_out, wout, wsem.at[1])
    wcopy_in.start()
    wcopy_out.start()

    wide[RAW:, :] = jnp.zeros((PAD * 32 - RAW, 128), F32)

    def extract(kind, dst):
        for n in range(4):
            fetch(kind, n).wait()
            rows = slice(n * (RAW // 4), (n + 1) * (RAW // 4))
            wide[rows, :] = raw[kind, rows, :].astype(F32)
        for a in range(8):
            dst[:, a * 128 : (a + 1) * 128] = wide[
                pl.ds(a * 4 + group, PAD, stride=32), :
            ].astype(BF)

    with scope("extract0"):
        extract(0, tok)
    router_copy.wait()
    logits = dot(tok[...], router[...], 1, 0)
    keep = lax.broadcasted_iota(jnp.int32, (PAD, S), 0) < TOK
    top = jnp.max(jnp.where(keep, logits, -jnp.inf), axis=0, keepdims=True)
    e = jnp.where(keep, jnp.exp(jnp.where(keep, logits - top, 0.0)), 0.0)
    disp[...] = e / jnp.sum(e, axis=0, keepdims=True)
    e = jnp.exp(logits - jnp.max(logits, axis=1, keepdims=True))
    comb[...] = e / jnp.sum(e, axis=1, keepdims=True)

    def to_tiles(kind, weights, values):
        flipped = weights.T.astype(BF)
        val = dot(flipped, values[...], 1, 0)
        for a in range(8):
            fs[pl.ds(a, S, stride=8), :] = val[:, a * 128 : (a + 1) * 128]
        sbuf[kind] = fs[...].reshape(S, 8, 128).astype(BF)

    def send_stage(st, h):
        kind, ex = st // 2, st % 2

        def send(i2, g2, r):
            pltpu.make_async_remote_copy(
                sbuf.at[kind, i2 * 2 + ex], x.at[st, 0, r], send1, recv1.at[st, h],
                device_id=dev(g2, i2),
            ).start()

        if h == NEAR:
            pltpu.make_async_copy(
                sbuf.at[kind, inner * 2 + ex], x.at[st, 0, SELF], recv1.at[st, h]
            ).start()
        each_peer(send, h)

    with scope("tiles0"):
        to_tiles(0, disp[...], tok)
    with scope("extract1"):
        extract(1, og)
    with scope("tiles1"):
        to_tiles(1, comb[...], og)
    with scope("barrier"):
        pl.semaphore_wait(barrier, NI - 1 + 3)
    with scope("send"):
        for st in range(4):
            for h in (NEAR, FAR) if st == 0 else (FAR, NEAR):
                send_stage(st, h)

    def part(st, q, h):
        return x.at[st, q, pl.ds(h * 32, 32)]

    def ycopy(st, h):
        return pltpu.make_async_remote_copy(
            part(st, 0, h), part(st, 1, h), ysend, yrecv.at[st, h],
            device_id=dev(quad(2), inner),
        )

    def ccopy(st, q, h):
        return pltpu.make_async_remote_copy(
            part(st, q, h), part(st, q + 2, h), csend, crecv.at[st, q],
            device_id=dev(quad(1), inner),
        )

    def forward_a(st, h):
        with scope(f"fwdA{st}{h}"):
            pltpu.make_async_copy(part(st, 0, h), part(st, 0, h), recv1.at[st, h]).wait()
        ycopy(st, h).start()
        ccopy(st, 0, h).start()

    def forward_b(st, h):
        with scope(f"fwdB{st}{h}"):
            ycopy(st, h).wait_recv()
        ccopy(st, 1, h).start()

    def to_rows(st, q):
        fs[0:512, :] = x[st, q].astype(F32).reshape(512, 128)
        for a in range(8):
            lhs[st, q * 64 : (q + 1) * 64, a * 128 : (a + 1) * 128] = fs[
                pl.ds(a, 64, stride=8), :
            ].astype(BF)

    def rows_ab(st):
        to_rows(st, 0)
        to_rows(st, 1)

    def rows_cd(st):
        for q in range(2):
            with scope(f"settle{st}{q}"):
                done = x.at[st, q + 2]
                pltpu.make_async_copy(done, done, crecv.at[st, q]).wait()
            to_rows(st, q + 2)

    def scatter_rows(dst, n, val):
        for q in range(4):
            for a in range(NT // 128):
                dst[pl.ds(q * 512 + n * (NT // 128) + a, 64, stride=8), :] = val[
                    q * 64 : (q + 1) * 64, a * 128 : (a + 1) * 128
                ]

    sums = (s0, s1, s2, s3)
    c0 = math.sqrt(2.0 / math.pi)

    def pre(ex):
        for n in range(D // NT):
            cols = slice(n * NT, (n + 1) * NT)
            h = dot(lhs[ex], win[ex, :, cols], 1, 0)
            h2 = h * h
            th = jnp.tanh(c0 * (h + 0.044715 * h2 * h))
            half = 0.5 * (1.0 + th)
            act[:, cols] = (h * half).astype(BF)
            dg[ex, :, cols] = half + 0.5 * h * (1.0 - th * th) * (
                c0 * (1.0 + (3.0 * 0.044715) * h2)
            )

    def out(ex):
        for n in range(D // NT):
            scatter_rows(sums[ex], n, dot(act[...], wout[ex, :, n * NT : (n + 1) * NT], 1, 0))

    def act_grad(ex):
        for n in range(D // NT):
            cols = slice(n * NT, (n + 1) * NT)
            ag = dot(lhs[2 + ex], wout[ex, cols, :], 1, 1)
            pg[:, cols] = (dg[ex, :, cols] * ag).astype(BF)

    def back(ex):
        for n in range(D // NT):
            scatter_rows(
                sums[2 + ex], n, dot(pg[...], win[ex, n * NT : (n + 1) * NT, :], 1, 1)
            )

    def pcopy(st, q):
        return pltpu.make_async_remote_copy(
            cbuf.at[st, q], pbuf.at[st, q], psend, precv.at[st, q],
            device_id=dev(quad(1), inner),
        )

    def bcopy(st, h):
        sel = pl.ds(h * 32, 32)
        return pltpu.make_async_remote_copy(
            ybuf.at[st, sel], rbuf.at[st, sel], bsend, brecv.at[st, h],
            device_id=dev(quad(2), inner),
        )

    def rows_of(st, q, h):
        lo = q * 512 + h * 256
        return sums[st][lo : lo + 256, :].reshape(32, 8, 128)

    def reduce_1(st):
        with scope(f"reduce1_{st}"):
            for q in (1, 0):
                cbuf[st, q] = (
                    sums[st][(q + 2) * 512 : (q + 3) * 512, :].reshape(64, 8, 128).astype(BF)
                )
                pcopy(st, q).start()

    def reduce_2(st):
        with scope(f"reduce2_{st}"):
            pcopy(st, 1).wait_recv()
            for h in (FAR, NEAR):
                sel = pl.ds(h * 32, 32)
                ybuf[st, sel] = (rows_of(st, 1, h) + pbuf[st, 1, sel].astype(F32)).astype(BF)
                bcopy(st, h).start()

    def reduce_3(st, h):
        kind, ex = st // 2, st % 2
        sel = pl.ds(h * 32, 32)
        with scope(f"reduce3_{st}{h}"):
            if h == FAR:
                pcopy(st, 0).wait_recv()
            bcopy(st, h).wait_recv()
        abuf[st, sel] = (
            rows_of(st, 0, h) + pbuf[st, 0, sel].astype(F32) + rbuf[st, sel].astype(F32)
        ).astype(BF)
        if h == NEAR:
            pltpu.make_async_copy(
                abuf.at[st, SELF], so.at[kind, inner, ex], arecv.at[kind]
            ).start()

        def send(i2, g2, r):
            pltpu.make_async_remote_copy(
                abuf.at[st, r], so.at[kind, inner, ex], asend, arecv.at[kind],
                device_id=dev(g2, i2),
            ).start()

        with scope("a2a"):
            each_peer(send, h, back=True)

    forward_a(0, NEAR)
    forward_a(0, FAR)
    forward_a(1, NEAR)
    forward_b(0, NEAR)
    forward_a(1, FAR)
    forward_b(0, FAR)
    with scope("rows"):
        rows_ab(0)
    forward_a(2, NEAR)
    with scope("rows"):
        rows_cd(0)
    wcopy_in.wait()
    wcopy_out.wait()
    with scope("pre"):
        pre(0)
    forward_b(1, NEAR)
    forward_a(2, FAR)
    forward_b(1, FAR)
    with scope("out"):
        out(0)
    reduce_1(0)
    forward_a(3, NEAR)
    with scope("rows"):
        rows_ab(1)
        rows_cd(1)
    forward_a(3, FAR)
    reduce_2(0)
    with scope("pre"):
        pre(1)
    forward_b(2, NEAR)
    forward_b(2, FAR)
    with scope("out"):
        out(1)
    reduce_1(1)
    with scope("rows"):
        rows_ab(2)
        rows_cd(2)
    with scope("actgrad"):
        act_grad(0)
    forward_b(3, NEAR)
    reduce_2(1)
    forward_b(3, FAR)
    with scope("back"):
        back(0)
    reduce_1(2)
    with scope("rows"):
        rows_ab(3)
        rows_cd(3)
    reduce_3(0, FAR)
    with scope("actgrad"):
        act_grad(1)
    reduce_2(2)
    reduce_3(0, NEAR)
    with scope("back"):
        back(1)
    reduce_1(3)
    reduce_3(1, FAR)
    reduce_2(3)
    reduce_3(1, NEAR)
    for st in (2, 3):
        for h in (FAR, NEAR):
            reduce_3(st, h)

    def gather_rows(kind):
        pltpu.make_async_copy(so.at[kind], so.at[kind], arecv.at[kind]).wait()
        fs[...] = so[kind].astype(F32).reshape(1024, 128)
        for a in range(8):
            so_m[kind, :, a * 128 : (a + 1) * 128] = fs[pl.ds(a, S, stride=8), :].astype(BF)

    with scope("gather0"):
        gather_rows(0)
    cg = dot(og[...], so_m[0], 1, 1)
    cw = comb[...]
    lg = cw * (cg - jnp.sum(cw * cg, axis=1, keepdims=True))
    with scope("gather1"):
        gather_rows(1)
    dgr = dot(tok[...], so_m[1], 1, 1)
    dw = disp[...]
    lg = lg + dw * (dgr - jnp.sum(dw * dgr, axis=0, keepdims=True))
    lb = lg.astype(BF)
    rgo[...] = dot(tok[...], lb, 0, 0).reshape(NI, 2, 8, 128)
    rgs[...] = rgo[:, pl.ds(1 - core, 1)].reshape(NI, 8, 128).astype(BF)

    gcopy = pltpu.make_async_remote_copy(
        rgs, rgp, gsend, grecv, device_id=dev(quad(1), inner)
    )
    gcopy.start()
    with scope("tg"):
        tg = dot(dw.astype(BF), so_m[1], 1, 0) + dot(lb, router[...], 1, 1)
        for g in range(4):
            tgb[g] = tg[:, g * 256 : (g + 1) * 256].astype(BF)

    def tcopy(j):
        g2 = quad(j)
        return pltpu.make_async_remote_copy(
            tgb.at[g2], land.at[group], tsend, trecv, device_id=dev(g2, inner)
        )

    for j in (2, 3, 1):
        tcopy(j).start()
    mine = pltpu.make_async_copy(tgb.at[group], land.at[group], trecv)
    mine.start()

    with scope("wait_g"):
        gcopy.wait_recv()
    rgb[...] = (
        rgo[:, pl.ds(core, 1)].reshape(NI, 8, 128) + rgp[...].astype(F32)
    ).astype(BF)

    def send_router(i2, g2, r):
        pltpu.make_async_remote_copy(
            rgb.at[i2], rr.at[r], rsend, rrecv, device_id=dev(g2, i2)
        ).start()

    with scope("send_router"):
        each_peer(send_router, FAR)
        each_peer(send_router, NEAR)
        pltpu.make_async_copy(rgb.at[inner], rr.at[SELF], rrecv).start()

    with scope("wait_tg"):
        pltpu.make_async_copy(land, land, trecv).wait()
    with scope("tg_out"):
        for g in range(4):
            for a in range(2):
                wide[pl.ds(a * 4 + g, PAD, stride=8), :] = land[
                    g, :, a * 128 : (a + 1) * 128
                ].astype(F32)
        tg_out[...] = wide[: TOK * 8, :].astype(BF)

    with scope("wait_router"):
        pltpu.make_async_copy(rr, rr, rrecv).wait()
    qs[0] = jnp.sum(rr[...].astype(F32), axis=0)

    def qcopy(j):
        return pltpu.make_async_remote_copy(
            qs.at[0], qs.at[j], qsend, qrecv, device_id=dev(quad(j), inner)
        )

    for j in (2, 3, 1):
        qcopy(j).start()
    with scope("wait_q"):
        pltpu.make_async_copy(qs.at[pl.ds(1, 3)], qs.at[pl.ds(1, 3)], qrecv).wait()
    rg[pl.ds(core * 8, 8), :] = qs[0] + qs[2]
    rg[pl.ds((1 - core) * 8, 8), :] = qs[1] + qs[3]

    with scope("end"):
        for ref, sem in (
            (x.at[:, 0, pl.ds(1, NI - 1)], send1),
            (abuf.at[:, pl.ds(1, NI - 1)], asend),
            (x.at[:, 0], ysend),
            (x.at[:, pl.ds(0, 2)], csend),
            (pbuf, psend),
            (rbuf, bsend),
            (rgp, gsend),
            (rr.at[pl.ds(1, NI - 1)], rsend),
            (land.at[pl.ds(0, 3)], tsend),
            (qs.at[pl.ds(1, 3)], qsend),
        ):
            pltpu.make_async_copy(ref, ref, sem).wait()


def finish(tg, rg, tg_out, rg_out, sem):
    rows = TOK * 8 // 4
    copies = [
        pltpu.make_async_copy(
            tg.at[pl.ds(n * rows, rows)], tg_out.at[pl.ds(n * rows, rows)], sem.at[n]
        )
        for n in range(4)
    ] + [pltpu.make_async_copy(rg, rg_out, sem.at[4])]
    for c in copies:
        c.start()
    for c in copies:
        c.wait()


def local(tokens, output_grad, router, weight_in, weight_out):
    def as_stored(a):
        a = a.transpose(1, 0, 2).reshape(TOK, 4, 8, 128).transpose(0, 2, 1, 3)
        return a.reshape(RAW, 128)

    dma = pltpu.SemaphoreType.DMA
    vm = pl.BlockSpec(memory_space=pltpu.VMEM)
    hbm = pl.BlockSpec(memory_space=pl.ANY)
    tg, rg = pl.pallas_call(
        kernel,
        name="moe_backward",
        out_shape=(pltpu.VMEM((TOK * 8, 128), BF), pltpu.VMEM((16, S), F32)),
        in_specs=[hbm, hbm, hbm, hbm, hbm],
        out_specs=(vm, vm),
        scratch_shapes=[
            pltpu.VMEM((2, RAW, 128), BF),
            pltpu.VMEM((PAD * 32, 128), F32),
            pltpu.VMEM((PAD, D), BF),
            pltpu.VMEM((PAD, D), BF),
            pltpu.VMEM((D, S), BF),
            pltpu.VMEM((4, PAD, 256), BF),
            pltpu.VMEM((2, D, D), BF),
            pltpu.VMEM((2, D, D), BF),
            pltpu.VMEM((PAD, S), F32),
            pltpu.VMEM((PAD, S), F32),
            pltpu.VMEM((2, S, 8, 128), BF),
            pltpu.VMEM((4, 4, NI, 8, 128), BF),
            pltpu.VMEM((1024, 128), F32),
            pltpu.VMEM((4, 256, D), BF),
            pltpu.VMEM((2, 256, D), F32),
            pltpu.VMEM((256, D), BF),
            pltpu.VMEM((256, D), BF),
            pltpu.VMEM((2048, 128), F32),
            pltpu.VMEM((2048, 128), F32),
            pltpu.VMEM((2048, 128), F32),
            pltpu.VMEM((2048, 128), F32),
            pltpu.VMEM((4, 2, NI, 8, 128), BF),
            pltpu.VMEM((4, 2, NI, 8, 128), BF),
            pltpu.VMEM((4, NI, 8, 128), BF),
            pltpu.VMEM((4, NI, 8, 128), BF),
            pltpu.VMEM((4, NI, 8, 128), BF),
            pltpu.VMEM((2, NI, 2, 8, 128), BF),
            pltpu.VMEM((2, S, D), BF),
            pltpu.VMEM((NI, 2, 8, 128), F32),
            pltpu.VMEM((NI, 8, 128), BF),
            pltpu.VMEM((NI, 8, 128), BF),
            pltpu.VMEM((NI, 8, 128), BF),
            pltpu.VMEM((NI, 8, 128), BF),
            pltpu.VMEM((4, PAD, 256), BF),
            pltpu.VMEM((4, 8, 128), F32),
            dma((2, 4)),
            dma((3,)),
            dma, dma((4, 2)),
            dma, dma((4, 2)),
            dma, dma((4, 2)),
            dma, dma((4, 2)),
            dma, dma((4, 2)),
            dma, dma((2,)),
            dma, dma,
            dma, dma,
            dma, dma,
            dma, dma,
        ],
        compiler_params=pltpu.CompilerParams(
            collective_id=0, has_side_effects=True, vmem_limit_bytes=58 * 1024 * 1024
        ),
    )(as_stored(tokens), as_stored(output_grad), router, weight_in, weight_out)
    tg, rg = pl.pallas_call(
        finish,
        name="moe_finish",
        out_shape=(
            jax.ShapeDtypeStruct((TOK * 8, 128), BF),
            jax.ShapeDtypeStruct((16, S), F32),
        ),
        in_specs=[vm, vm],
        out_specs=(hbm, hbm),
        scratch_shapes=[dma((5,))],
        compiler_params=pltpu.CompilerParams(vmem_limit_bytes=8 * 1024 * 1024),
    )(tg, rg)
    tg = tg.reshape(TOK, 2, 4, 128).transpose(2, 0, 1, 3).reshape(4, TOK, 256)
    return tg, rg


def solution(mesh):
    return jax.shard_map(
        local,
        mesh=mesh,
        in_specs=(
            P("inner", None, None),
            P("inner", None, None),
            P(),
            P("inner", None, "group"),
            P("inner", "group", None),
        ),
        out_specs=(P("inner", None, "group"), P("inner", None)),
        check_vma=False,
    )
```

```python
import contextlib
import math

import jax
import jax.numpy as jnp
from jax import lax
from jax.experimental import pallas as pl
from jax.experimental.pallas import tpu as pltpu
from jax.sharding import PartitionSpec as P

BF = jnp.bfloat16
F32 = jnp.float32
NX, NZ, NY = 4, 8, 2
NI = NX * NZ * NY
TOK = 196
PAD = 208
D = 1024
S = 128
RAW = TOK * 32
NT = 512
NEAR, FAR = 0, 1
DZ = ((0, 1, 7, 2), (4, 3, 5, 6))
SELF = 0


def scope(name):
    return contextlib.nullcontext()


def dot(a, b, ca, cb):
    return lax.dot_general(a, b, (((ca,), (cb,)), ((), ())), preferred_element_type=F32)


def kernel(
    tok_all, og_all, router_all, w_in, w_out,
    tg_out, rg,
    raw, wide, tok, og, router, land, tok_t, win, wout, disp, comb, sbuf, x, fs, lhs, dg, act, pg, s0, s1, s2, s3,
    cbuf, pbuf, ybuf, rbuf, abuf, so, so_m, rgo, rgs, rgp, rgb, rr, tgb, qs,
    tsem, wsem, send1, recv1, ysend, yrecv, csend, crecv,
    psend, precv, bsend, brecv, asend, arecv,
    gsend, grecv, rsend, rrecv, qsend, qrecv, tsend, trecv,
):
    inner = lax.axis_index("inner")
    group = lax.axis_index("group")
    yh = lax.rem(inner, NY)
    zc = lax.rem(lax.div(inner, NY), NZ)
    xc = lax.div(inner, NY * NZ)
    yl = lax.div(group, 2)
    core = lax.rem(group, 2)

    ahead = [lax.rem(zc + dz, NZ) * NY for dz in range(NZ)]
    behind = [lax.rem(zc + NZ - dz, NZ) * NY for dz in range(NZ)]

    def each_peer(fn, half, back=False, down=False):
        def at(t, js):
            dx, dy = lax.rem(t, NX), lax.div(t, NX)
            x2 = lax.rem(xc + (NX - dx if back else dx), NX) * (NY * NZ)
            y2, l2 = lax.rem(yh + dy, 2), lax.rem(yl + dy, 2)
            base, g2 = x2 + y2, l2 * 2 + core
            for j in js:
                dz = DZ[half][j]
                fn(base + (behind if back else ahead)[dz], g2, half * 32 + j * 8 + t)

        lo = 0
        if half == NEAR:
            at(jnp.int32(0), (1, 2, 3))
            lo = 1

        @pl.loop(lo, 8)
        def _(t):
            at(lo + 7 - t if down else t, (0, 1, 2, 3))

    def quad(j):
        return lax.rem(yl + j // 2, 2) * 2 + lax.rem(core + j % 2, 2)

    def dev(g, i):
        return {"group": g, "inner": i}

    def fetch(kind, n):
        src = (tok_all, og_all)[kind]
        rows = pl.ds(n * (RAW // 4), RAW // 4)
        return pltpu.make_async_copy(src.at[rows], raw.at[kind, rows], tsem.at[kind, n])

    router_copy = pltpu.make_async_copy(router_all, router, wsem.at[2])
    for n in range(4):
        fetch(0, n).start()
    router_copy.start()
    for n in range(4):
        fetch(1, n).start()
    barrier = pltpu.get_barrier_semaphore()

    def greet(i2, g2, r):
        pl.semaphore_signal(barrier, inc=1, device_id=dev(g2, i2))

    each_peer(greet, FAR, down=True)
    each_peer(greet, NEAR, down=True)
    for j in range(1, 4):
        pl.semaphore_signal(barrier, inc=1, device_id=dev(quad(j), inner))

    wcopy_in = pltpu.make_async_copy(w_in, win, wsem.at[0])
    wcopy_out = pltpu.make_async_copy(w_out, wout, wsem.at[1])
    wcopy_in.start()
    wcopy_out.start()

    wide[RAW:, :] = jnp.zeros((PAD * 32 - RAW, 128), F32)

    def extract(kind, dst):
        for n in range(4):
            fetch(kind, n).wait()
            rows = slice(n * (RAW // 4), (n + 1) * (RAW // 4))
            wide[rows, :] = raw[kind, rows, :].astype(F32)
        for a in range(8):
            dst[:, a * 128 : (a + 1) * 128] = wide[
                pl.ds(a * 4 + group, PAD, stride=32), :
            ].astype(BF)

    with scope("extract0"):
        extract(0, tok)
    router_copy.wait()
    logits = dot(tok[...], router[...], 1, 0)
    keep = lax.broadcasted_iota(jnp.int32, (PAD, S), 0) < TOK
    top = jnp.max(jnp.where(keep, logits, -jnp.inf), axis=0, keepdims=True)
    e = jnp.where(keep, jnp.exp(jnp.where(keep, logits - top, 0.0)), 0.0)
    disp[...] = e / jnp.sum(e, axis=0, keepdims=True)
    e = jnp.exp(logits - jnp.max(logits, axis=1, keepdims=True))
    comb[...] = e / jnp.sum(e, axis=1, keepdims=True)

    def to_tiles(kind, weights, values):
        flipped = weights.T.astype(BF)
        val = dot(flipped, values[...], 1, 0)
        for a in range(8):
            fs[pl.ds(a, S, stride=8), :] = val[:, a * 128 : (a + 1) * 128]
        sbuf[kind] = fs[...].reshape(S, 8, 128).astype(BF)

    def send_stage(st, h):
        kind, ex = st // 2, st % 2

        def send(i2, g2, r):
            pltpu.make_async_remote_copy(
                sbuf.at[kind, i2 * 2 + ex], x.at[st, 0, r], send1, recv1.at[st, h],
                device_id=dev(g2, i2),
            ).start()

        if h == NEAR:
            pltpu.make_async_copy(
                sbuf.at[kind, inner * 2 + ex], x.at[st, 0, SELF], recv1.at[st, h]
            ).start()
        each_peer(send, h)

    with scope("tiles0"):
        to_tiles(0, disp[...], tok)
    with scope("extract1"):
        extract(1, og)
    with scope("tiles1"):
        to_tiles(1, comb[...], og)
    with scope("barrier"):
        pl.semaphore_wait(barrier, NI - 1 + 3)
    with scope("send"):
        for st in range(4):
            for h in (NEAR, FAR) if st == 0 else (FAR, NEAR):
                send_stage(st, h)

    def part(st, q, h):
        return x.at[st, q, pl.ds(h * 32, 32)]

    def ycopy(st, h):
        return pltpu.make_async_remote_copy(
            part(st, 0, h), part(st, 1, h), ysend, yrecv.at[st, h],
            device_id=dev(quad(2), inner),
        )

    def ccopy(st, q, h):
        return pltpu.make_async_remote_copy(
            part(st, q, h), part(st, q + 2, h), csend, crecv.at[st],
            device_id=dev(quad(1), inner),
        )

    def forward_a(st, h):
        with scope(f"fwdA{st}{h}"):
            pltpu.make_async_copy(part(st, 0, h), part(st, 0, h), recv1.at[st, h]).wait()
        ycopy(st, h).start()
        ccopy(st, 0, h).start()

    def forward_b(st, h):
        with scope(f"fwdB{st}{h}"):
            ycopy(st, h).wait_recv()
        ccopy(st, 1, h).start()

    def to_rows(st, q):
        fs[0:512, :] = x[st, q].astype(F32).reshape(512, 128)
        for a in range(8):
            lhs[st, q * 64 : (q + 1) * 64, a * 128 : (a + 1) * 128] = fs[
                pl.ds(a, 64, stride=8), :
            ].astype(BF)

    def rows_ab(st):
        to_rows(st, 0)
        to_rows(st, 1)

    def rows_cd(st):
        with scope(f"settle{st}"):
            done = x.at[st, pl.ds(2, 2)]
            pltpu.make_async_copy(done, done, crecv.at[st]).wait()
        for q in range(2):
            to_rows(st, q + 2)

    def scatter_rows(dst, n, val):
        for q in range(4):
            for a in range(NT // 128):
                dst[pl.ds(q * 512 + n * (NT // 128) + a, 64, stride=8), :] = val[
                    q * 64 : (q + 1) * 64, a * 128 : (a + 1) * 128
                ]

    sums = (s0, s1, s2, s3)
    c0 = math.sqrt(2.0 / math.pi)

    def pre(ex):
        for n in range(D // NT):
            cols = slice(n * NT, (n + 1) * NT)
            h = dot(lhs[ex], win[ex, :, cols], 1, 0)
            h2 = h * h
            th = jnp.tanh(c0 * (h + 0.044715 * h2 * h))
            half = 0.5 * (1.0 + th)
            act[:, cols] = (h * half).astype(BF)
            dg[ex, :, cols] = half + 0.5 * h * (1.0 - th * th) * (
                c0 * (1.0 + (3.0 * 0.044715) * h2)
            )

    def out(ex):
        for n in range(D // NT):
            scatter_rows(sums[ex], n, dot(act[...], wout[ex, :, n * NT : (n + 1) * NT], 1, 0))

    def act_grad(ex):
        for n in range(D // NT):
            cols = slice(n * NT, (n + 1) * NT)
            ag = dot(lhs[2 + ex], wout[ex, cols, :], 1, 1)
            pg[:, cols] = (dg[ex, :, cols] * ag).astype(BF)

    def back(ex):
        for n in range(D // NT):
            scatter_rows(
                sums[2 + ex], n, dot(pg[...], win[ex, n * NT : (n + 1) * NT, :], 1, 1)
            )

    def pcopy(st, q):
        return pltpu.make_async_remote_copy(
            cbuf.at[st, q], pbuf.at[st, q], psend, precv.at[st, q],
            device_id=dev(quad(1), inner),
        )

    def bcopy(st, h):
        sel = pl.ds(h * 32, 32)
        return pltpu.make_async_remote_copy(
            ybuf.at[st, sel], rbuf.at[st, sel], bsend, brecv.at[st, h],
            device_id=dev(quad(2), inner),
        )

    def rows_of(st, q, h):
        lo = q * 512 + h * 256
        return sums[st][lo : lo + 256, :].reshape(32, 8, 128)

    def reduce_1(st):
        with scope(f"reduce1_{st}"):
            for q in (1, 0):
                cbuf[st, q] = (
                    sums[st][(q + 2) * 512 : (q + 3) * 512, :].reshape(64, 8, 128).astype(BF)
                )
                pcopy(st, q).start()

    def reduce_2(st, halves=(FAR, NEAR), first=True):
        with scope(f"reduce2_{st}"):
            if first:
                pcopy(st, 1).wait_recv()
            for h in halves:
                sel = pl.ds(h * 32, 32)
                ybuf[st, sel] = (rows_of(st, 1, h) + pbuf[st, 1, sel].astype(F32)).astype(BF)
                bcopy(st, h).start()

    def reduce_3(st, h):
        kind, ex = st // 2, st % 2
        sel = pl.ds(h * 32, 32)
        with scope(f"reduce3_{st}{h}"):
            if h == FAR:
                pcopy(st, 0).wait_recv()
            bcopy(st, h).wait_recv()
        abuf[st, sel] = (
            rows_of(st, 0, h) + pbuf[st, 0, sel].astype(F32) + rbuf[st, sel].astype(F32)
        ).astype(BF)
        if h == NEAR:
            pltpu.make_async_copy(
                abuf.at[st, SELF], so.at[kind, inner, ex], arecv.at[kind]
            ).start()

        def send(i2, g2, r):
            pltpu.make_async_remote_copy(
                abuf.at[st, r], so.at[kind, inner, ex], asend, arecv.at[kind],
                device_id=dev(g2, i2),
            ).start()

        with scope("a2a"):
            each_peer(send, h, back=True)

    with scope("tok_t"):
        for a in range(8):
            turned = tok[:, a * 128 : (a + 1) * 128].astype(F32).T.reshape(8, 2, 8, PAD)
            for half in range(2):
                tok_t[half, a * 64 : (a + 1) * 64, :] = (
                    turned[:, half].reshape(64, PAD).astype(BF)
                )
    forward_a(0, NEAR)
    forward_a(0, FAR)
    forward_a(1, NEAR)
    forward_b(0, NEAR)
    forward_a(1, FAR)
    forward_b(0, FAR)
    with scope("rows"):
        rows_ab(0)
    forward_a(2, NEAR)
    with scope("rows"):
        rows_cd(0)
    wcopy_in.wait()
    wcopy_out.wait()
    with scope("pre"):
        pre(0)
    forward_b(1, NEAR)
    forward_a(2, FAR)
    forward_b(1, FAR)
    with scope("out"):
        out(0)
    reduce_1(0)
    forward_a(3, NEAR)
    with scope("rows"):
        rows_ab(1)
        rows_cd(1)
    forward_a(3, FAR)
    reduce_2(0)
    with scope("pre"):
        pre(1)
    forward_b(2, NEAR)
    forward_b(2, FAR)
    with scope("out"):
        out(1)
    reduce_1(1)
    with scope("rows"):
        rows_ab(2)
        rows_cd(2)
    with scope("actgrad"):
        act_grad(0)
    forward_b(3, NEAR)
    reduce_2(1)
    forward_b(3, FAR)
    with scope("back"):
        back(0)
    reduce_1(2)
    with scope("rows"):
        rows_ab(3)
        rows_cd(3)
    reduce_3(0, FAR)
    with scope("actgrad"):
        act_grad(1)
    reduce_2(2)
    reduce_3(0, NEAR)
    with scope("back"):
        back(1)
    reduce_1(3)
    reduce_3(1, FAR)
    reduce_2(3)
    reduce_3(1, NEAR)
    for st in (2, 3):
        for h in (FAR, NEAR):
            reduce_3(st, h)

    def gather_rows(kind):
        pltpu.make_async_copy(so.at[kind], so.at[kind], arecv.at[kind]).wait()
        fs[...] = so[kind].astype(F32).reshape(1024, 128)
        for a in range(8):
            so_m[kind, :, a * 128 : (a + 1) * 128] = fs[pl.ds(a, S, stride=8), :].astype(BF)

    with scope("gather0"):
        gather_rows(0)
    cg = dot(og[...], so_m[0], 1, 1)
    cw = comb[...]
    lg = cw * (cg - jnp.sum(cw * cg, axis=1, keepdims=True))
    with scope("gather1"):
        gather_rows(1)
    dgr = dot(tok[...], so_m[1], 1, 1)
    dw = disp[...]
    lg = lg + dw * (dgr - jnp.sum(dw * dgr, axis=0, keepdims=True))
    lb = lg.astype(BF)
    rgs[...] = dot(tok_t[1 - core], lb, 1, 0).reshape(NI, 8, 128).astype(BF)
    gcopy = pltpu.make_async_remote_copy(
        rgs, rgp, gsend, grecv, device_id=dev(quad(1), inner)
    )
    gcopy.start()
    rgo[...] = dot(tok_t[core], lb, 1, 0).reshape(NI, 8, 128)
    with scope("tg"):
        tg = dot(dw.astype(BF), so_m[1], 1, 0) + dot(lb, router[...], 1, 1)
        for g in range(4):
            tgb[g] = tg[:, g * 256 : (g + 1) * 256].astype(BF)

    def tcopy(j):
        g2 = quad(j)
        return pltpu.make_async_remote_copy(
            tgb.at[g2], land.at[group], tsend, trecv, device_id=dev(g2, inner)
        )

    for j in (2, 3, 1):
        tcopy(j).start()
    mine = pltpu.make_async_copy(tgb.at[group], land.at[group], trecv)
    mine.start()

    with scope("wait_g"):
        gcopy.wait_recv()
    rgb[...] = (rgo[...] + rgp[...].astype(F32)).astype(BF)

    def send_router(i2, g2, r):
        pltpu.make_async_remote_copy(
            rgb.at[i2], rr.at[r], rsend, rrecv, device_id=dev(g2, i2)
        ).start()

    with scope("send_router"):
        each_peer(send_router, FAR)
        each_peer(send_router, NEAR)
        pltpu.make_async_copy(rgb.at[inner], rr.at[SELF], rrecv).start()

    with scope("wait_tg"):
        pltpu.make_async_copy(land, land, trecv).wait()
    with scope("tg_out"):
        for g in range(4):
            for a in range(2):
                wide[pl.ds(a * 4 + g, PAD, stride=8), :] = land[
                    g, :, a * 128 : (a + 1) * 128
                ].astype(F32)
        tg_out[...] = wide[: TOK * 8, :].astype(BF)

    with scope("wait_router"):
        pltpu.make_async_copy(rr, rr, rrecv).wait()
    qs[0] = jnp.sum(rr[...].astype(F32), axis=0)

    def qcopy(j):
        return pltpu.make_async_remote_copy(
            qs.at[0], qs.at[j], qsend, qrecv, device_id=dev(quad(j), inner)
        )

    for j in (2, 3, 1):
        qcopy(j).start()
    with scope("wait_q"):
        pltpu.make_async_copy(qs.at[pl.ds(1, 3)], qs.at[pl.ds(1, 3)], qrecv).wait()
    rg[pl.ds(core * 8, 8), :] = qs[0] + qs[2]
    rg[pl.ds((1 - core) * 8, 8), :] = qs[1] + qs[3]

    with scope("end"):
        for ref, sem in (
            (x.at[:, 0, pl.ds(1, NI - 1)], send1),
            (abuf.at[:, pl.ds(1, NI - 1)], asend),
            (x.at[:, 0], ysend),
            (x.at[:, pl.ds(0, 2)], csend),
            (pbuf, psend),
            (rbuf, bsend),
            (rgp, gsend),
            (rr.at[pl.ds(1, NI - 1)], rsend),
            (land.at[pl.ds(0, 3)], tsend),
            (qs.at[pl.ds(1, 3)], qsend),
        ):
            pltpu.make_async_copy(ref, ref, sem).wait()


def finish(tg, rg, tg_out, rg_out, sem):
    rows = TOK * 8 // 4
    copies = [
        pltpu.make_async_copy(
            tg.at[pl.ds(n * rows, rows)], tg_out.at[pl.ds(n * rows, rows)], sem.at[n]
        )
        for n in range(4)
    ] + [pltpu.make_async_copy(rg, rg_out, sem.at[4])]
    for c in copies:
        c.start()
    for c in copies:
        c.wait()


def local(tokens, output_grad, router, weight_in, weight_out):
    def as_stored(a):
        a = a.transpose(1, 0, 2).reshape(TOK, 4, 8, 128).transpose(0, 2, 1, 3)
        return a.reshape(RAW, 128)

    dma = pltpu.SemaphoreType.DMA
    vm = pl.BlockSpec(memory_space=pltpu.VMEM)
    hbm = pl.BlockSpec(memory_space=pl.ANY)
    tg, rg = pl.pallas_call(
        kernel,
        name="moe_backward",
        out_shape=(pltpu.VMEM((TOK * 8, 128), BF), pltpu.VMEM((16, S), F32)),
        in_specs=[hbm, hbm, hbm, hbm, hbm],
        out_specs=(vm, vm),
        scratch_shapes=[
            pltpu.VMEM((2, RAW, 128), BF),
            pltpu.VMEM((PAD * 32, 128), F32),
            pltpu.VMEM((PAD, D), BF),
            pltpu.VMEM((PAD, D), BF),
            pltpu.VMEM((D, S), BF),
            pltpu.VMEM((4, PAD, 256), BF),
            pltpu.VMEM((2, D // 2, PAD), BF),
            pltpu.VMEM((2, D, D), BF),
            pltpu.VMEM((2, D, D), BF),
            pltpu.VMEM((PAD, S), F32),
            pltpu.VMEM((PAD, S), F32),
            pltpu.VMEM((2, S, 8, 128), BF),
            pltpu.VMEM((4, 4, NI, 8, 128), BF),
            pltpu.VMEM((1024, 128), F32),
            pltpu.VMEM((4, 256, D), BF),
            pltpu.VMEM((2, 256, D), F32),
            pltpu.VMEM((256, D), BF),
            pltpu.VMEM((256, D), BF),
            pltpu.VMEM((2048, 128), F32),
            pltpu.VMEM((2048, 128), F32),
            pltpu.VMEM((2048, 128), F32),
            pltpu.VMEM((2048, 128), F32),
            pltpu.VMEM((4, 2, NI, 8, 128), BF),
            pltpu.VMEM((4, 2, NI, 8, 128), BF),
            pltpu.VMEM((4, NI, 8, 128), BF),
            pltpu.VMEM((4, NI, 8, 128), BF),
            pltpu.VMEM((4, NI, 8, 128), BF),
            pltpu.VMEM((2, NI, 2, 8, 128), BF),
            pltpu.VMEM((2, S, D), BF),
            pltpu.VMEM((NI, 8, 128), F32),
            pltpu.VMEM((NI, 8, 128), BF),
            pltpu.VMEM((NI, 8, 128), BF),
            pltpu.VMEM((NI, 8, 128), BF),
            pltpu.VMEM((NI, 8, 128), BF),
            pltpu.VMEM((4, PAD, 256), BF),
            pltpu.VMEM((4, 8, 128), F32),
            dma((2, 4)),
            dma((3,)),
            dma, dma((4, 2)),
            dma, dma((4, 2)),
            dma, dma((4,)),
            dma, dma((4, 2)),
            dma, dma((4, 2)),
            dma, dma((2,)),
            dma, dma,
            dma, dma,
            dma, dma,
            dma, dma,
        ],
        compiler_params=pltpu.CompilerParams(
            collective_id=0, has_side_effects=True, vmem_limit_bytes=58 * 1024 * 1024
        ),
    )(as_stored(tokens), as_stored(output_grad), router, weight_in, weight_out)
    tg, rg = pl.pallas_call(
        finish,
        name="moe_finish",
        out_shape=(
            jax.ShapeDtypeStruct((TOK * 8, 128), BF),
            jax.ShapeDtypeStruct((16, S), F32),
        ),
        in_specs=[vm, vm],
        out_specs=(hbm, hbm),
        scratch_shapes=[dma((5,))],
        compiler_params=pltpu.CompilerParams(vmem_limit_bytes=8 * 1024 * 1024),
    )(tg, rg)
    tg = tg.reshape(TOK, 2, 4, 128).transpose(2, 0, 1, 3).reshape(4, TOK, 256)
    return tg, rg


def solution(mesh):
    return jax.shard_map(
        local,
        mesh=mesh,
        in_specs=(
            P("inner", None, None),
            P("inner", None, None),
            P(),
            P("inner", None, "group"),
            P("inner", "group", None),
        ),
        out_specs=(P("inner", None, "group"), P("inner", None)),
        check_vma=False,
    )
```

```python
import contextlib
import math

import jax
import jax.numpy as jnp
from jax import lax
from jax.experimental import pallas as pl
from jax.experimental.pallas import tpu as pltpu
from jax.sharding import PartitionSpec as P

BF = jnp.bfloat16
F32 = jnp.float32
NX, NZ, NY = 4, 8, 2
NI = NX * NZ * NY
TOK = 196
PAD = 208
D = 1024
S = 128
RAW = TOK * 32
NT = 512
NEAR, FAR = 0, 1
DZ = ((0, 1, 7, 2), (4, 3, 5, 6))
SELF = 0


def scope(name):
    return contextlib.nullcontext()


def dot(a, b, ca, cb):
    return lax.dot_general(a, b, (((ca,), (cb,)), ((), ())), preferred_element_type=F32)


def kernel(
    tok_all, og_all, router_all, w_in, w_out,
    tg_out, rg,
    raw, wide, tok, og, router, land, tok_t, win, wout, disp, comb, sbuf, x, fs, lhs, dg, act, pg, s0, s1, s2, s3,
    cbuf, pbuf, ybuf, rbuf, abuf, so, so_m, rgo, rgs, rgp, rgb, rr, tgb, qs,
    tsem, wsem, send1, recv1, ysend, yrecv, csend, crecv,
    psend, precv, bsend, brecv, asend, arecv,
    gsend, grecv, rsend, rrecv, qsend, qrecv, tsend, trecv,
):
    inner = lax.axis_index("inner")
    group = lax.axis_index("group")
    yh = lax.rem(inner, NY)
    zc = lax.rem(lax.div(inner, NY), NZ)
    xc = lax.div(inner, NY * NZ)
    yl = lax.div(group, 2)
    core = lax.rem(group, 2)

    ahead = [lax.rem(zc + dz, NZ) * NY for dz in range(NZ)]
    behind = [lax.rem(zc + NZ - dz, NZ) * NY for dz in range(NZ)]

    def each_peer(fn, half, back=False, down=False):
        def at(t, js):
            dx, dy = lax.rem(t, NX), lax.div(t, NX)
            x2 = lax.rem(xc + (NX - dx if back else dx), NX) * (NY * NZ)
            y2, l2 = lax.rem(yh + dy, 2), lax.rem(yl + dy, 2)
            base, g2 = x2 + y2, l2 * 2 + core
            for j in js:
                dz = DZ[half][j]
                fn(base + (behind if back else ahead)[dz], g2, half * 32 + j * 8 + t)

        lo = 0
        if half == NEAR:
            at(jnp.int32(0), (1, 2, 3))
            lo = 1

        @pl.loop(lo, 8)
        def _(t):
            at(lo + 7 - t if down else t, (0, 1, 2, 3))

    def quad(j):
        return lax.rem(yl + j // 2, 2) * 2 + lax.rem(core + j % 2, 2)

    def dev(g, i):
        return {"group": g, "inner": i}

    def fetch(kind, n):
        src = (tok_all, og_all)[kind]
        rows = pl.ds(n * (RAW // 4), RAW // 4)
        return pltpu.make_async_copy(src.at[rows], raw.at[kind, rows], tsem.at[kind, n])

    router_copy = pltpu.make_async_copy(router_all, router, wsem.at[2])
    for n in range(4):
        fetch(0, n).start()
    router_copy.start()
    for n in range(4):
        fetch(1, n).start()
    barrier = pltpu.get_barrier_semaphore()

    def greet(i2, g2, r):
        pl.semaphore_signal(barrier, inc=1, device_id=dev(g2, i2))

    each_peer(greet, FAR, down=True)
    each_peer(greet, NEAR, down=True)
    for j in range(1, 4):
        pl.semaphore_signal(barrier, inc=1, device_id=dev(quad(j), inner))

    wcopy_in = pltpu.make_async_copy(w_in, win, wsem.at[0])
    wcopy_out = pltpu.make_async_copy(w_out, wout, wsem.at[1])
    wcopy_in.start()
    wcopy_out.start()

    wide[RAW:, :] = jnp.zeros((PAD * 32 - RAW, 128), F32)

    def extract(kind, dst):
        for n in range(4):
            fetch(kind, n).wait()
            rows = slice(n * (RAW // 4), (n + 1) * (RAW // 4))
            wide[rows, :] = raw[kind, rows, :].astype(F32)
        for a in range(8):
            dst[:, a * 128 : (a + 1) * 128] = wide[
                pl.ds(a * 4 + group, PAD, stride=32), :
            ].astype(BF)

    with scope("extract0"):
        extract(0, tok)
    router_copy.wait()
    logits = dot(tok[...], router[...], 1, 0)
    keep = lax.broadcasted_iota(jnp.int32, (PAD, S), 0) < TOK
    top = jnp.max(jnp.where(keep, logits, -jnp.inf), axis=0, keepdims=True)
    e = jnp.where(keep, jnp.exp(jnp.where(keep, logits - top, 0.0)), 0.0)
    disp[...] = e / jnp.sum(e, axis=0, keepdims=True)
    e = jnp.exp(logits - jnp.max(logits, axis=1, keepdims=True))
    comb[...] = e / jnp.sum(e, axis=1, keepdims=True)

    def to_tiles(kind, weights, values):
        flipped = weights.T.astype(BF)
        val = dot(flipped, values[...], 1, 0)
        for a in range(8):
            fs[pl.ds(a, S, stride=8), :] = val[:, a * 128 : (a + 1) * 128]
        sbuf[kind] = fs[...].reshape(S, 8, 128).astype(BF)

    def send_stage(st, h):
        kind, ex = st // 2, st % 2

        def send(i2, g2, r):
            pltpu.make_async_remote_copy(
                sbuf.at[kind, i2 * 2 + ex], x.at[st, 0, r], send1, recv1.at[st, h],
                device_id=dev(g2, i2),
            ).start()

        if h == NEAR:
            pltpu.make_async_copy(
                sbuf.at[kind, inner * 2 + ex], x.at[st, 0, SELF], recv1.at[st, h]
            ).start()
        each_peer(send, h)

    with scope("tiles0"):
        to_tiles(0, disp[...], tok)
    with scope("extract1"):
        extract(1, og)
    with scope("tiles1"):
        to_tiles(1, comb[...], og)
    with scope("barrier"):
        pl.semaphore_wait(barrier, NI - 1 + 3)
    with scope("send"):
        for st in range(4):
            for h in (NEAR, FAR) if st < 3 else (FAR, NEAR):
                send_stage(st, h)

    def part(st, q, h):
        return x.at[st, q, pl.ds(h * 32, 32)]

    def ycopy(st, h):
        return pltpu.make_async_remote_copy(
            part(st, 0, h), part(st, 1, h), ysend, yrecv.at[st, h],
            device_id=dev(quad(2), inner),
        )

    def ccopy(st, q, h):
        return pltpu.make_async_remote_copy(
            part(st, q, h), part(st, q + 2, h), csend, crecv.at[st],
            device_id=dev(quad(1), inner),
        )

    def forward_a(st, h):
        with scope(f"fwdA{st}{h}"):
            pltpu.make_async_copy(part(st, 0, h), part(st, 0, h), recv1.at[st, h]).wait()
        ycopy(st, h).start()
        ccopy(st, 0, h).start()

    def forward_b(st, h):
        with scope(f"fwdB{st}{h}"):
            ycopy(st, h).wait_recv()
        ccopy(st, 1, h).start()

    def to_rows(st, q):
        fs[0:512, :] = x[st, q].astype(F32).reshape(512, 128)
        for a in range(8):
            lhs[st, q * 64 : (q + 1) * 64, a * 128 : (a + 1) * 128] = fs[
                pl.ds(a, 64, stride=8), :
            ].astype(BF)

    def rows_ab(st):
        to_rows(st, 0)
        to_rows(st, 1)

    def rows_cd(st):
        with scope(f"settle{st}"):
            done = x.at[st, pl.ds(2, 2)]
            pltpu.make_async_copy(done, done, crecv.at[st]).wait()
        for q in range(2):
            to_rows(st, q + 2)

    def scatter_rows(dst, n, val):
        for q in range(4):
            for a in range(NT // 128):
                dst[pl.ds(q * 512 + n * (NT // 128) + a, 64, stride=8), :] = val[
                    q * 64 : (q + 1) * 64, a * 128 : (a + 1) * 128
                ]

    sums = (s0, s1, s2, s3)
    c0 = math.sqrt(2.0 / math.pi)

    def pre(ex):
        for n in range(D // NT):
            cols = slice(n * NT, (n + 1) * NT)
            h = dot(lhs[ex], win[ex, :, cols], 1, 0)
            h2 = h * h
            th = jnp.tanh(c0 * (h + 0.044715 * h2 * h))
            half = 0.5 * (1.0 + th)
            act[:, cols] = (h * half).astype(BF)
            dg[ex, :, cols] = half + 0.5 * h * (1.0 - th * th) * (
                c0 * (1.0 + (3.0 * 0.044715) * h2)
            )

    def out(ex):
        for n in range(D // NT):
            scatter_rows(sums[ex], n, dot(act[...], wout[ex, :, n * NT : (n + 1) * NT], 1, 0))

    def act_grad(ex):
        for n in range(D // NT):
            cols = slice(n * NT, (n + 1) * NT)
            ag = dot(lhs[2 + ex], wout[ex, cols, :], 1, 1)
            pg[:, cols] = (dg[ex, :, cols] * ag).astype(BF)

    def back(ex):
        for n in range(D // NT):
            scatter_rows(
                sums[2 + ex], n, dot(pg[...], win[ex, n * NT : (n + 1) * NT, :], 1, 1)
            )

    def pcopy(st, q):
        return pltpu.make_async_remote_copy(
            cbuf.at[st, q], pbuf.at[st, q], psend, precv.at[st, q],
            device_id=dev(quad(1), inner),
        )

    def bcopy(st, h):
        sel = pl.ds(h * 32, 32)
        return pltpu.make_async_remote_copy(
            ybuf.at[st, sel], rbuf.at[st, sel], bsend, brecv.at[st, h],
            device_id=dev(quad(2), inner),
        )

    def rows_of(st, q, h):
        lo = q * 512 + h * 256
        return sums[st][lo : lo + 256, :].reshape(32, 8, 128)

    def reduce_1(st):
        with scope(f"reduce1_{st}"):
            for q in (1, 0):
                cbuf[st, q] = (
                    sums[st][(q + 2) * 512 : (q + 3) * 512, :].reshape(64, 8, 128).astype(BF)
                )
                pcopy(st, q).start()

    def reduce_2(st, halves=(FAR, NEAR), first=True):
        with scope(f"reduce2_{st}"):
            if first:
                pcopy(st, 1).wait_recv()
            for h in halves:
                sel = pl.ds(h * 32, 32)
                ybuf[st, sel] = (rows_of(st, 1, h) + pbuf[st, 1, sel].astype(F32)).astype(BF)
                bcopy(st, h).start()

    def reduce_3(st, h):
        kind, ex = st // 2, st % 2
        sel = pl.ds(h * 32, 32)
        with scope(f"reduce3_{st}{h}"):
            if h == FAR:
                pcopy(st, 0).wait_recv()
            bcopy(st, h).wait_recv()
        abuf[st, sel] = (
            rows_of(st, 0, h) + pbuf[st, 0, sel].astype(F32) + rbuf[st, sel].astype(F32)
        ).astype(BF)
        if h == NEAR:
            pltpu.make_async_copy(
                abuf.at[st, SELF], so.at[kind, inner, ex], arecv.at[kind]
            ).start()

        def send(i2, g2, r):
            pltpu.make_async_remote_copy(
                abuf.at[st, r], so.at[kind, inner, ex], asend, arecv.at[kind],
                device_id=dev(g2, i2),
            ).start()

        with scope("a2a"):
            each_peer(send, h, back=True)

    with scope("tok_t"):
        for a in range(8):
            turned = tok[:, a * 128 : (a + 1) * 128].astype(F32).T.reshape(8, 2, 8, PAD)
            for half in range(2):
                tok_t[half, a * 64 : (a + 1) * 64, :] = (
                    turned[:, half].reshape(64, PAD).astype(BF)
                )
    forward_a(0, NEAR)
    forward_a(0, FAR)
    forward_a(1, NEAR)
    forward_b(0, NEAR)
    forward_a(1, FAR)
    forward_b(0, FAR)
    with scope("rows"):
        rows_ab(0)
    forward_a(2, NEAR)
    with scope("rows"):
        rows_cd(0)
    wcopy_in.wait()
    wcopy_out.wait()
    with scope("pre"):
        pre(0)
    forward_b(1, NEAR)
    forward_a(2, FAR)
    forward_b(1, FAR)
    with scope("out"):
        out(0)
    reduce_1(0)
    forward_a(3, NEAR)
    with scope("rows"):
        rows_ab(1)
        rows_cd(1)
    forward_a(3, FAR)
    reduce_2(0)
    with scope("pre"):
        pre(1)
    forward_b(2, NEAR)
    forward_b(2, FAR)
    with scope("out"):
        out(1)
    reduce_1(1)
    with scope("rows"):
        rows_ab(2)
        rows_cd(2)
    with scope("actgrad"):
        act_grad(0)
    forward_b(3, NEAR)
    reduce_2(1)
    forward_b(3, FAR)
    with scope("back"):
        back(0)
    reduce_1(2)
    with scope("rows"):
        rows_ab(3)
        rows_cd(3)
    with scope("actgrad"):
        act_grad(1)
    reduce_3(0, FAR)
    reduce_2(2)
    reduce_3(0, NEAR)
    with scope("back"):
        back(1)
    reduce_1(3)
    reduce_3(1, FAR)
    reduce_2(3)
    reduce_3(1, NEAR)
    for st in (2, 3):
        for h in (FAR, NEAR):
            reduce_3(st, h)

    def gather_rows(kind):
        pltpu.make_async_copy(so.at[kind], so.at[kind], arecv.at[kind]).wait()
        fs[...] = so[kind].astype(F32).reshape(1024, 128)
        for a in range(8):
            so_m[kind, :, a * 128 : (a + 1) * 128] = fs[pl.ds(a, S, stride=8), :].astype(BF)

    with scope("gather0"):
        gather_rows(0)
    cg = dot(og[...], so_m[0], 1, 1)
    cw = comb[...]
    lg = cw * (cg - jnp.sum(cw * cg, axis=1, keepdims=True))
    with scope("gather1"):
        gather_rows(1)
    dgr = dot(tok[...], so_m[1], 1, 1)
    dw = disp[...]
    lg = lg + dw * (dgr - jnp.sum(dw * dgr, axis=0, keepdims=True))
    lb = lg.astype(BF)
    rgs[...] = dot(tok_t[1 - core], lb, 1, 0).reshape(NI, 8, 128).astype(BF)
    gcopy = pltpu.make_async_remote_copy(
        rgs, rgp, gsend, grecv, device_id=dev(quad(1), inner)
    )
    gcopy.start()
    rgo[...] = dot(tok_t[core], lb, 1, 0).reshape(NI, 8, 128)
    with scope("tg"):
        tg = dot(dw.astype(BF), so_m[1], 1, 0) + dot(lb, router[...], 1, 1)
        for g in range(4):
            tgb[g] = tg[:, g * 256 : (g + 1) * 256].astype(BF)

    def tcopy(j):
        g2 = quad(j)
        return pltpu.make_async_remote_copy(
            tgb.at[g2], land.at[group], tsend, trecv, device_id=dev(g2, inner)
        )

    for j in (2, 3, 1):
        tcopy(j).start()
    mine = pltpu.make_async_copy(tgb.at[group], land.at[group], trecv)
    mine.start()

    with scope("wait_g"):
        gcopy.wait_recv()
    rgb[...] = (rgo[...] + rgp[...].astype(F32)).astype(BF)

    def send_router(i2, g2, r):
        pltpu.make_async_remote_copy(
            rgb.at[i2], rr.at[r], rsend, rrecv, device_id=dev(g2, i2)
        ).start()

    with scope("send_router"):
        each_peer(send_router, FAR)
        each_peer(send_router, NEAR)
        pltpu.make_async_copy(rgb.at[inner], rr.at[SELF], rrecv).start()

    with scope("wait_tg"):
        pltpu.make_async_copy(land, land, trecv).wait()
    with scope("tg_out"):
        for g in range(4):
            for a in range(2):
                wide[pl.ds(a * 4 + g, PAD, stride=8), :] = land[
                    g, :, a * 128 : (a + 1) * 128
                ].astype(F32)
        tg_out[...] = wide[: TOK * 8, :].astype(BF)

    with scope("wait_router"):
        pltpu.make_async_copy(rr, rr, rrecv).wait()
    qs[0] = jnp.sum(rr[...].astype(F32), axis=0)

    def qcopy(j):
        return pltpu.make_async_remote_copy(
            qs.at[0], qs.at[j], qsend, qrecv, device_id=dev(quad(j), inner)
        )

    for j in (2, 3, 1):
        qcopy(j).start()
    with scope("wait_q"):
        pltpu.make_async_copy(qs.at[pl.ds(1, 3)], qs.at[pl.ds(1, 3)], qrecv).wait()
    rg[pl.ds(core * 8, 8), :] = qs[0] + qs[2]
    rg[pl.ds((1 - core) * 8, 8), :] = qs[1] + qs[3]

    with scope("end"):
        for ref, sem in (
            (x.at[:, 0, pl.ds(1, NI - 1)], send1),
            (abuf.at[:, pl.ds(1, NI - 1)], asend),
            (x.at[:, 0], ysend),
            (x.at[:, pl.ds(0, 2)], csend),
            (pbuf, psend),
            (rbuf, bsend),
            (rgp, gsend),
            (rr.at[pl.ds(1, NI - 1)], rsend),
            (land.at[pl.ds(0, 3)], tsend),
            (qs.at[pl.ds(1, 3)], qsend),
        ):
            pltpu.make_async_copy(ref, ref, sem).wait()


def finish(tg, rg, tg_out, rg_out, sem):
    rows = TOK * 8 // 4
    copies = [
        pltpu.make_async_copy(
            tg.at[pl.ds(n * rows, rows)], tg_out.at[pl.ds(n * rows, rows)], sem.at[n]
        )
        for n in range(4)
    ] + [pltpu.make_async_copy(rg, rg_out, sem.at[4])]
    for c in copies:
        c.start()
    for c in copies:
        c.wait()


def local(tokens, output_grad, router, weight_in, weight_out):
    def as_stored(a):
        a = a.transpose(1, 0, 2).reshape(TOK, 4, 8, 128).transpose(0, 2, 1, 3)
        return a.reshape(RAW, 128)

    dma = pltpu.SemaphoreType.DMA
    vm = pl.BlockSpec(memory_space=pltpu.VMEM)
    hbm = pl.BlockSpec(memory_space=pl.ANY)
    tg, rg = pl.pallas_call(
        kernel,
        name="moe_backward",
        out_shape=(pltpu.VMEM((TOK * 8, 128), BF), pltpu.VMEM((16, S), F32)),
        in_specs=[hbm, hbm, hbm, hbm, hbm],
        out_specs=(vm, vm),
        scratch_shapes=[
            pltpu.VMEM((2, RAW, 128), BF),
            pltpu.VMEM((PAD * 32, 128), F32),
            pltpu.VMEM((PAD, D), BF),
            pltpu.VMEM((PAD, D), BF),
            pltpu.VMEM((D, S), BF),
            pltpu.VMEM((4, PAD, 256), BF),
            pltpu.VMEM((2, D // 2, PAD), BF),
            pltpu.VMEM((2, D, D), BF),
            pltpu.VMEM((2, D, D), BF),
            pltpu.VMEM((PAD, S), F32),
            pltpu.VMEM((PAD, S), F32),
            pltpu.VMEM((2, S, 8, 128), BF),
            pltpu.VMEM((4, 4, NI, 8, 128), BF),
            pltpu.VMEM((1024, 128), F32),
            pltpu.VMEM((4, 256, D), BF),
            pltpu.VMEM((2, 256, D), F32),
            pltpu.VMEM((256, D), BF),
            pltpu.VMEM((256, D), BF),
            pltpu.VMEM((2048, 128), F32),
            pltpu.VMEM((2048, 128), F32),
            pltpu.VMEM((2048, 128), F32),
            pltpu.VMEM((2048, 128), F32),
            pltpu.VMEM((4, 2, NI, 8, 128), BF),
            pltpu.VMEM((4, 2, NI, 8, 128), BF),
            pltpu.VMEM((4, NI, 8, 128), BF),
            pltpu.VMEM((4, NI, 8, 128), BF),
            pltpu.VMEM((4, NI, 8, 128), BF),
            pltpu.VMEM((2, NI, 2, 8, 128), BF),
            pltpu.VMEM((2, S, D), BF),
            pltpu.VMEM((NI, 8, 128), F32),
            pltpu.VMEM((NI, 8, 128), BF),
            pltpu.VMEM((NI, 8, 128), BF),
            pltpu.VMEM((NI, 8, 128), BF),
            pltpu.VMEM((NI, 8, 128), BF),
            pltpu.VMEM((4, PAD, 256), BF),
            pltpu.VMEM((4, 8, 128), F32),
            dma((2, 4)),
            dma((3,)),
            dma, dma((4, 2)),
            dma, dma((4, 2)),
            dma, dma((4,)),
            dma, dma((4, 2)),
            dma, dma((4, 2)),
            dma, dma((2,)),
            dma, dma,
            dma, dma,
            dma, dma,
            dma, dma,
        ],
        compiler_params=pltpu.CompilerParams(
            collective_id=0, has_side_effects=True, vmem_limit_bytes=58 * 1024 * 1024
        ),
    )(as_stored(tokens), as_stored(output_grad), router, weight_in, weight_out)
    tg, rg = pl.pallas_call(
        finish,
        name="moe_finish",
        out_shape=(
            jax.ShapeDtypeStruct((TOK * 8, 128), BF),
            jax.ShapeDtypeStruct((16, S), F32),
        ),
        in_specs=[vm, vm],
        out_specs=(hbm, hbm),
        scratch_shapes=[dma((5,))],
        compiler_params=pltpu.CompilerParams(vmem_limit_bytes=8 * 1024 * 1024),
    )(tg, rg)
    tg = tg.reshape(TOK, 2, 4, 128).transpose(2, 0, 1, 3).reshape(4, TOK, 256)
    return tg, rg


def solution(mesh):
    return jax.shard_map(
        local,
        mesh=mesh,
        in_specs=(
            P("inner", None, None),
            P("inner", None, None),
            P(),
            P("inner", None, "group"),
            P("inner", "group", None),
        ),
        out_specs=(P("inner", None, "group"), P("inner", None)),
        check_vma=False,
    )
```
